32 devices in a mesh: dp: 4 (over y, x), label: 8 (over z, core).
Axes of the slice: x: 2, y: 2, z: 4, core: 2. Of those that a mesh axis runs over, the one named last changes fastest.
Arguments:
- samples: bfloat16 [4096, 4096], P(('dp', 'label')), may hold values from -6 to 6
- weight: bfloat16 [4096, 16, 256], P('dp', 'label'), may hold values from -0.09375 to 0.09375
- matches: int32 [4096, 8], P(('dp', 'label')), may hold values from 0 to 15, all different within a row; in each aligned block of 128 rows (0 to 127, 128 to 255, ...) at most 128 rows name the same one
- positives: int32 [4096, 8], P(('dp', 'label')), may hold values from 0 to 255
Outputs:
- weight_grad: bfloat16 [4096, 16, 256], P('dp', 'label')
- sample_loss: float32 [4096], P(('dp', 'label'))
The draws below stay inside these ranges and needn't reach their ends.
Inputs may be any that keep to these rules, and one draw needn't show every extreme that they name: `matches`: each sample names 8 different clusters; among the 128 samples of one device (aligned blocks of rows) no cluster is named by more than 128 samples, a bound that some block reaches.
All inputs are finite; a program needn't handle non-finite values.
Results may differ from the reference program's by a relative error of at most 0.0043.
Values may be sent and summed in bfloat16 or wider, within the bound.
No kernel may reach another device: no remote copies, remote signals or barrier semaphores. Data moves between devices by JAX's collectives and lax.ppermute only.
A program may use at most 128 MiB of HBM per device.

```python
import math
import jax
import jax.numpy as jnp
import numpy as np
from jax import lax

D = 4096
LABELS = 256
MATCHES = 8
SAMP_DEV = 128
CLUSTERS = 16
CAP = 128
SAMPLES = 4096
DEVICES = 32


def set_ends(drawn, stream_key, smallest, high):
    dims = drawn.shape
    spot = [jax.random.randint(jax.random.fold_in(stream_key, axis), (), 0, dims[axis]) for axis in range(len(dims))]
    drawn = drawn.at[tuple(spot)].set(smallest)
    longest = dims.index(max(dims))
    spot[longest] = (spot[longest] + 1) % dims[longest]
    return drawn.at[tuple(spot)].set(high)


def levels(stream_key, extent, split, least, high):
    gain, own = 1.0, jax.random.fold_in(stream_key, 6)
    for position, parts in split:
        steps = jnp.exp(jax.random.uniform(jax.random.fold_in(own, position), (parts,), jnp.float32, least / len(split), high / len(split)))
        gain = gain * jnp.repeat(steps, extent[position] // parts).reshape([-1 if axis == position else 1 for axis in range(len(extent))])
    return gain


def assign_block(stream_key, own, number, rows, amount, top, reach, slope):
    ranking = jax.random.permutation(stream_key, amount)
    packed, usual = shares(amount, rows * top, reach, slope, True), shares(amount, rows * top, reach, slope, False)
    places = jnp.arange(amount)

    def named(sizes, rotation):
        used = int((sizes > 0).sum())
        fixed = max(1, used // 4)
        passed = fixed + (places - fixed + rotation * (used - fixed)) % max(1, amount - fixed)
        return jnp.zeros((amount,), jnp.int32).at[ranking[jnp.where(places < fixed, places, passed)]].set(jnp.asarray(sizes, jnp.int32))

    sizes = jnp.where(number % 4 == 0, named(packed, number // 4), named(usual, number - number // 4 - 1))
    mixed = jax.random.permutation(jax.random.fold_in(own, 3), amount)
    donor, receiver = mixed[0:amount // 2 * 2:2], mixed[1:amount // 2 * 2:2]
    margin = jnp.minimum(sizes[donor] - 1, reach - sizes[receiver]) // 2
    margin = jnp.where((donor == ranking[0]) | (receiver == ranking[0]) | (sizes[receiver] == 0), 0, jnp.maximum(margin, 0))
    passed = jax.random.randint(jax.random.fold_in(own, 4), (amount // 2,), 0, 1 << 20) % (margin + 1)
    sizes = sizes.at[donor].add(-passed).at[receiver].add(passed)
    items = jnp.searchsorted(jnp.cumsum(sizes), jnp.arange(rows * top), side="right").astype(jnp.int32)
    grid = items.reshape(top, rows).T
    grid = grid[jax.random.permutation(jax.random.fold_in(own, 1), rows)]
    rotation = jax.random.randint(jax.random.fold_in(own, 2), (rows, 1), 0, top)
    return jnp.take_along_axis(grid, (jnp.arange(top)[None, :] + rotation) % top, axis=1)


def shares(amount, total, reach, lean, full):
    loads = [(1 << 20) // math.isqrt(rank ** lean) + 1 for rank in range(1, amount + 1)]
    largest = reach if full else min(reach, max(-(-total // amount), total * loads[0] // sum(loads)))
    least = 1 if total - largest >= amount - 1 else 0
    counts, surplus = [largest] + [least] * (amount - 1), total - largest - least * (amount - 1)
    while surplus > 0:
        movable = [i for i in range(1, amount) if counts[i] < largest] or [i for i in range(1, amount) if counts[i] < reach]
        pool, budget = sum([loads[i] for i in movable]), surplus
        for i in movable:
            addition = min(reach - counts[i], max(1, budget * loads[i] // pool), surplus)
            counts[i] = counts[i] + addition
            surplus = surplus - addition
    return np.array(counts)


def centred(own_key, extent, deviation, most, split=(), held_as=jnp.bfloat16):
    values = jax.random.normal(own_key, extent, jnp.float32) * deviation
    if len(split) > 0:
        values = levels(own_key, extent, split, -0.22, 0.18) * values
    return jnp.clip(values, min=-most, max=most).astype(held_as)


def setup_inputs(seed: int = 0) -> dict:
    splits = jax.random.split(jax.random.key(seed), 5)
    samples = centred(splits[0], (SAMPLES, D), 1.0, 6.0, ((0, 32),))
    weight = centred(splits[1], (D, CLUSTERS, LABELS), D ** -0.5, 0.09375, ((0, 4), (1, 8)))
    matches_keys = jax.random.split(jax.random.fold_in(splits[2], 1), SAMPLES // SAMP_DEV)
    matches_turns = jax.random.permutation(jax.random.fold_in(splits[2], 3), SAMPLES // SAMP_DEV)
    matches = jax.vmap(lambda own, number: assign_block(jax.random.fold_in(splits[2], 2), own, number, SAMP_DEV, CLUSTERS, MATCHES, CAP, 2))(matches_keys, matches_turns).reshape((SAMPLES, MATCHES))
    positives = set_ends(jax.random.randint(splits[3], (SAMPLES, MATCHES), 0, LABELS), jax.random.fold_in(splits[3], 1), 0, LABELS - 1).astype(jnp.int32)
    return {"samples": samples, "weight": weight, "matches": matches, "positives": positives}


inv_temp = 2.0
grad_scale = 0.03125


def slot_terms(scores, labels):
    logits = scores * inv_temp
    label_ids = jnp.arange(scores.shape[-1], dtype=jnp.int32)
    targets = (label_ids == labels[..., None]).astype(jnp.float32)
    valid_mask = (labels >= 0).astype(jnp.float32)[..., None]
    per_label = jnp.maximum(logits, 0.0) + jnp.log1p(jnp.exp(-jnp.abs(logits))) - targets * logits
    slot_loss = jnp.sum(per_label * valid_mask, axis=-1)
    gradients = ((jax.nn.sigmoid(logits) - targets) * (inv_temp * grad_scale) * valid_mask).astype(jnp.bfloat16)
    return slot_loss, gradients


def reference(samples, weight, matches, positives):
    total_rows = samples.shape[0]
    pick_count = matches.shape[1]
    clusters = weight.shape[1]
    label_count = weight.shape[2]
    room = DEVICES * CAP
    flat_ids = matches.reshape(-1).astype(jnp.int32)
    onehot = (flat_ids[:, None] == jnp.arange(clusters, dtype=jnp.int32)[None, :]).astype(jnp.int32)
    rank_ids = jnp.sum((jnp.cumsum(onehot, axis=0) - 1) * onehot, axis=1).astype(jnp.int32)
    slot_ids = flat_ids * room + rank_ids
    owners = (jnp.arange(flat_ids.shape[0], dtype=jnp.int32) // pick_count).astype(jnp.int32)
    slot_row = jnp.zeros((clusters * room,), jnp.int32).at[slot_ids].set(owners).reshape(clusters, room)
    slot_label = jnp.full((clusters * room,), -1, jnp.int32).at[slot_ids].set(positives.reshape(-1).astype(jnp.int32)).reshape(clusters, room)

    def one_cluster(inputs):
        cluster_rows, cluster_labels, cluster_weight = inputs
        sel_rows = samples[cluster_rows]
        scores = jnp.dot(sel_rows, cluster_weight, preferred_element_type=jnp.float32)
        slot_loss, gradients = slot_terms(scores, cluster_labels)
        cluster_grad = jnp.dot(sel_rows.T, gradients, preferred_element_type=jnp.float32)
        return slot_loss, cluster_grad

    slot_loss, grad_stack = lax.map(one_cluster, (slot_row, slot_label, jnp.transpose(weight, (1, 0, 2))))
    weight_grad = jnp.transpose(grad_stack, (1, 0, 2)).astype(jnp.bfloat16)
    per_match = slot_loss.reshape(-1)[slot_ids].reshape(total_rows, pick_count)
    sample_loss = jnp.sum(per_match, axis=1) / (pick_count * label_count)
    return weight_grad, sample_loss
```

```python
import functools

import jax
import jax.numpy as jnp
from jax import lax
from jax.experimental import pallas as pl
from jax.experimental.pallas import tpu as pltpu
from jax.sharding import PartitionSpec as P

inv_temp = 2.0
grad_scale = 0.03125

ring_next = (1, 3, 0, 2)
ring_prev = (2, 0, 3, 1)
halves = 2


def slot_tables(matches, positives, clusters, capacity):
    row_count, pick_count = matches.shape
    flat_ids = matches.reshape(row_count * pick_count)
    onehot = (flat_ids[:, None] == jnp.arange(clusters, dtype=jnp.int32)[None, :]).astype(jnp.int32)
    rank_ids = jnp.sum((jnp.cumsum(onehot, axis=0) - 1) * onehot, axis=1)
    slot_ids = flat_ids * capacity + rank_ids
    owners = jnp.arange(row_count * pick_count, dtype=jnp.int32) // pick_count
    slot_row = jnp.zeros((clusters * capacity,), jnp.int32).at[slot_ids].set(owners)
    slot_label = (
        jnp.full((clusters * capacity,), -1, jnp.int32)
        .at[slot_ids]
        .set(positives.reshape(row_count * pick_count))
    )
    return (slot_ids, slot_row, slot_label.reshape(clusters, capacity))


def slot_terms(scores, labels):
    logits = scores * inv_temp
    label_ids = jnp.arange(scores.shape[-1], dtype=jnp.int32)
    targets = (label_ids == labels[..., None]).astype(jnp.float32)
    valid_mask = (labels >= 0).astype(jnp.float32)[..., None]
    per_label = jnp.maximum(logits, 0.0) + jnp.log1p(jnp.exp(-jnp.abs(logits))) - targets * logits
    slot_loss = jnp.sum(per_label * valid_mask, axis=-1)
    gradients = ((jax.nn.sigmoid(logits) - targets) * (inv_temp * grad_scale) * valid_mask).astype(
        jnp.bfloat16
    )
    return (slot_loss, gradients)


def slot_body(samples, weight, matches, positives):
    row_count, feat_width = samples.shape
    groups = lax.axis_size("label")
    local_count = weight.shape[1]
    label_count = weight.shape[2]
    clusters = groups * local_count
    pick_count = matches.shape[1]
    capacity = 2 * row_count * pick_count // clusters
    slot_ids, slot_row, slot_label = slot_tables(matches, positives, clusters, capacity)
    outgoing = samples[slot_row].reshape(clusters, capacity, feat_width)
    incoming, labels = (
        lax.all_to_all(outgoing, "label", split_axis=0, concat_axis=0, tiled=True),
        lax.all_to_all(slot_label, "label", split_axis=0, concat_axis=0, tiled=True),
    )
    incoming = incoming.reshape(groups, local_count, capacity, feat_width)
    labels = labels.reshape(groups, local_count, capacity)
    scores = jnp.einsum(
        "scpd,dcl->scpl",
        incoming,
        lax.all_gather(weight, "dp", axis=0, tiled=True),
        preferred_element_type=jnp.float32,
    )
    slot_loss, gradients = slot_terms(scores, labels)
    weight_grad = lax.psum_scatter(
        jnp.einsum("scpd,scpl->dcl", incoming, gradients, preferred_element_type=jnp.float32),
        "dp",
        scatter_dimension=0,
        tiled=True,
    ).astype(jnp.bfloat16)
    returned = lax.all_to_all(
        slot_loss.reshape(clusters, -1), "label", split_axis=0, concat_axis=0, tiled=True
    )
    per_match = returned.reshape(-1)[slot_ids].reshape(row_count, pick_count)
    sample_loss = jnp.sum(per_match, axis=1) / (pick_count * label_count)
    return (weight_grad, sample_loss)


def score_kernel(blocks, local_count, me_ref, *refs):
    xs, ws, code_ref = refs[:blocks], refs[blocks : blocks + 4], refs[blocks + 4]
    grad_ref, loss_ref = refs[blocks + 5 :]
    me = me_ref[0]
    depth, columns = ws[0].shape
    scores = None
    for offset in range(4):
        start = pl.multiple_of((me ^ offset) * depth, depth)
        rows = jnp.concatenate([x[:, pl.ds(start, depth)] for x in xs], axis=0)
        part = jnp.dot(rows, ws[offset][...], preferred_element_type=jnp.float32)
        scores = part if scores is None else scores + part
    label_count = columns // local_count
    label_ids = lax.broadcasted_iota(jnp.int32, (scores.shape[0], label_count), 1) + 1
    loss = None
    for cluster in range(local_count):
        span = slice(cluster * label_count, (cluster + 1) * label_count)
        code = code_ref[:, cluster : cluster + 1]
        logits = scores[:, span] * inv_temp
        hit = label_ids == code
        decay = jnp.exp(-jnp.abs(logits))
        each = jnp.maximum(logits, 0.0) + jnp.log1p(decay) - jnp.where(hit, logits, 0.0)
        share = jnp.where(logits >= 0.0, 1.0, decay) / (1.0 + decay)
        valid = code > 0
        grad = (share - jnp.where(hit, 1.0, 0.0)) * (inv_temp * grad_scale)
        grad_ref[:, span] = jnp.where(valid, grad, 0.0).astype(jnp.bfloat16)
        sums = jnp.where(valid, jnp.sum(each, axis=1, keepdims=True), 0.0)
        loss = sums if loss is None else loss + sums
    loss_ref[...] = loss


def score_call(me, xs, ws, codes):
    rows = sum(x.shape[0] for x in xs)
    feat_width = xs[0].shape[1]
    columns = ws[0].shape[1]
    whole = pl.BlockSpec(memory_space=pltpu.VMEM)
    return pl.pallas_call(
        functools.partial(score_kernel, len(xs), codes.shape[1]),
        out_shape=(
            jax.ShapeDtypeStruct((rows, columns), jnp.bfloat16),
            jax.ShapeDtypeStruct((rows, 1), jnp.float32),
        ),
        in_specs=[pl.BlockSpec(memory_space=pltpu.SMEM)] + [whole] * (len(xs) + 5),
        out_specs=(whole, whole),
        compiler_params=pltpu.CompilerParams(vmem_limit_bytes=32 << 20),
        cost_estimate=pl.CostEstimate(
            flops=2 * rows * feat_width * columns,
            bytes_accessed=2 * (rows + columns) * feat_width,
            transcendentals=2 * rows * columns,
        ),
        name="scores",
    )(me, *xs, *ws, codes)


def grad_kernel(counts, outs, me_ref, *refs):
    blocks = sum(counts)
    xs, gs = refs[:blocks], refs[blocks : blocks + len(counts)]
    out_refs = refs[blocks + len(counts) :]
    total = None
    at = 0
    for count, g in zip(counts, gs):
        rows = jnp.concatenate([x[...] for x in xs[at : at + count]], axis=0)
        at += count
        part = lax.dot_general(
            rows, g[...], (((0,), (0,)), ((), ())), preferred_element_type=jnp.float32
        )
        total = part if total is None else total + part
    width = total.shape[1] // outs
    for place in range(outs):
        out_refs[place][...] = total[:, place * width : (place + 1) * width].astype(
            out_refs[place].dtype
        )


def grad_call(me, offset, depth, groups_x, gs, kinds):
    xs = [x for group in groups_x for x in group]
    counts = [len(group) for group in groups_x]
    columns = gs[0].shape[1]
    rows = sum(g.shape[0] for g in gs)
    width = columns // len(kinds)
    steps = 4
    tile = depth // steps
    whole = pl.BlockSpec(memory_space=pltpu.VMEM)
    return pl.pallas_call(
        functools.partial(grad_kernel, counts, len(kinds)),
        out_shape=tuple(jax.ShapeDtypeStruct((depth, width), kind) for kind in kinds),
        grid_spec=pltpu.PrefetchScalarGridSpec(
            num_scalar_prefetch=1,
            grid=(steps,),
            in_specs=[
                pl.BlockSpec(
                    (x.shape[0], tile), lambda i, me_ref: (0, (me_ref[0] ^ offset) * steps + i)
                )
                for x in xs
            ]
            + [pl.BlockSpec(g.shape, lambda i, me_ref: (0, 0)) for g in gs],
            out_specs=tuple(pl.BlockSpec((tile, width), lambda i, me_ref: (i, 0)) for _ in kinds),
        ),
        compiler_params=pltpu.CompilerParams(vmem_limit_bytes=32 << 20),
        cost_estimate=pl.CostEstimate(
            flops=2 * rows * depth * columns,
            bytes_accessed=2 * rows * (depth + columns) + 3 * depth * columns,
            transcendentals=0,
        ),
        name="grads",
    )(me, *xs, *gs)


def ring_body(samples, weight, matches, positives):
    row_count, feat_width = samples.shape
    depth, local_count, label_count = weight.shape
    groups = lax.axis_size("label")
    pick_count = matches.shape[1]
    clusters = groups * local_count
    dp = lax.axis_index("dp")
    label = lax.axis_index("label")
    me = dp.reshape(1).astype(jnp.int32)

    chips = groups // 2
    hop = [(z * 2 + c, ring_next[z] * 2 + c) for z in range(chips) for c in range(2)]
    swap = [(i, i ^ 1) for i in range(groups)]
    along_x = [(i, i ^ 1) for i in range(4)]
    along_y = [(i, i ^ 2) for i in range(4)]
    diagonal = [(i, i ^ 3) for i in range(4)]

    part = row_count // halves
    mine = [[samples[h * part : (h + 1) * part] for h in range(halves)]]
    for step in range(1, chips):
        mine.append([lax.ppermute(b, "label", hop) for b in mine[-1]])
    mate = [[lax.ppermute(b, "label", swap) for b in row] for row in mine]

    flat = weight.reshape(depth, local_count * label_count)
    ws = [
        flat,
        lax.ppermute(flat, "dp", along_x),
        lax.ppermute(flat, "dp", along_y),
        lax.ppermute(flat, "dp", diagonal),
    ]

    cluster_ids = jnp.arange(clusters, dtype=jnp.int32)[:, None, None]
    code = jnp.sum(
        jnp.where(matches.T[None] == cluster_ids, positives.T[None] + 1, 0), axis=1
    ).reshape(groups, local_count, row_count)
    code = lax.all_to_all(code, "label", split_axis=0, concat_axis=0, tiled=True)

    order = []
    for z in range(chips):
        for c in range(2):
            at, rows = z, []
            for _ in range(chips):
                rows.append([at * 2 + c, at * 2 + 1 - c])
                at = ring_prev[at]
            order.append(rows)
    order = jnp.array(order, jnp.int32)[label]
    code = jnp.transpose(code[order], (0, 1, 3, 2))

    groups_x, gs, losses = [], [], []
    for step in range(chips):
        pieces = [range(halves)] if step < chips - 1 else [[h] for h in range(halves)]
        for piece in pieces:
            xs = [mine[step][h] for h in piece] + [mate[step][h] for h in piece]
            span = slice(piece[0] * part, (piece[-1] + 1) * part)
            codes = code[step, :, span].reshape(-1, local_count)
            grad, loss = score_call(me, xs, ws, codes)
            groups_x.append(xs)
            gs.append(grad)
            losses.append((step, span, loss.reshape(2, -1)))

    far = grad_call(me, 3, depth, groups_x, gs, (jnp.bfloat16, jnp.bfloat16))
    far_x = lax.ppermute(far[0], "dp", along_x)
    far_y = lax.ppermute(far[1], "dp", along_y)
    near_x = grad_call(me, 1, depth, groups_x, gs, (jnp.bfloat16, jnp.float32))
    got_x = lax.ppermute(near_x[0], "dp", along_x)
    near_y = grad_call(me, 2, depth, groups_x, gs, (jnp.float32, jnp.bfloat16))
    got_y = lax.ppermute(near_y[1], "dp", along_y)
    own = grad_call(me, 0, depth, groups_x, gs, (jnp.float32, jnp.float32))
    pass_y = lax.ppermute((near_y[0] + far_x).astype(jnp.bfloat16), "dp", along_y)
    pass_x = lax.ppermute((near_x[1] + far_y).astype(jnp.bfloat16), "dp", along_x)

    total = jnp.zeros((groups, row_count), jnp.float32)
    by_step = jnp.concatenate(
        [
            jnp.concatenate([loss for at, _, loss in losses if at == step], axis=1)
            for step in range(chips)
        ],
        axis=0,
    )
    total = total.at[order.reshape(-1)].set(by_step)
    returned = lax.all_to_all(total, "label", split_axis=0, concat_axis=0, tiled=True)
    sample_loss = jnp.sum(returned, axis=0) / (pick_count * label_count)

    first = own[0] + got_x.astype(jnp.float32) + pass_y.astype(jnp.float32)
    second = own[1] + got_y.astype(jnp.float32) + pass_x.astype(jnp.float32)
    weight_grad = jnp.stack([first, second], axis=1).astype(jnp.bfloat16)
    return (weight_grad, sample_loss)


def body(samples, weight, matches, positives):
    if (lax.axis_size("dp"), lax.axis_size("label"), weight.shape[1]) == (4, 8, 2):
        return ring_body(samples, weight, matches, positives)
    return slot_body(samples, weight, matches, positives)


def solution(mesh):
    placed = (
        P(("dp", "label"), None),
        P("dp", "label", None),
        P(("dp", "label"), None),
        P(("dp", "label"), None),
    )
    return jax.shard_map(
        body,
        mesh=mesh,
        in_specs=placed,
        out_specs=(P("dp", "label", None), P(("dp", "label"))),
        check_vma=False,
    )
```

```python
import functools

import jax
import jax.numpy as jnp
from jax import lax
from jax.experimental import pallas as pl
from jax.experimental.pallas import tpu as pltpu
from jax.sharding import PartitionSpec as P

inv_temp = 2.0
grad_scale = 0.03125

ring_next = (1, 3, 0, 2)
ring_prev = (2, 0, 3, 1)
kernel_vmem = 58 << 20
lanes = 128


def slot_tables(matches, positives, clusters, capacity):
    row_count, pick_count = matches.shape
    flat_ids = matches.reshape(row_count * pick_count)
    onehot = (flat_ids[:, None] == jnp.arange(clusters, dtype=jnp.int32)[None, :]).astype(jnp.int32)
    rank_ids = jnp.sum((jnp.cumsum(onehot, axis=0) - 1) * onehot, axis=1)
    slot_ids = flat_ids * capacity + rank_ids
    owners = jnp.arange(row_count * pick_count, dtype=jnp.int32) // pick_count
    slot_row = jnp.zeros((clusters * capacity,), jnp.int32).at[slot_ids].set(owners)
    slot_label = (
        jnp.full((clusters * capacity,), -1, jnp.int32)
        .at[slot_ids]
        .set(positives.reshape(row_count * pick_count))
    )
    return (slot_ids, slot_row, slot_label.reshape(clusters, capacity))


def slot_terms(scores, labels):
    logits = scores * inv_temp
    label_ids = jnp.arange(scores.shape[-1], dtype=jnp.int32)
    targets = (label_ids == labels[..., None]).astype(jnp.float32)
    valid_mask = (labels >= 0).astype(jnp.float32)[..., None]
    per_label = jnp.maximum(logits, 0.0) + jnp.log1p(jnp.exp(-jnp.abs(logits))) - targets * logits
    slot_loss = jnp.sum(per_label * valid_mask, axis=-1)
    gradients = ((jax.nn.sigmoid(logits) - targets) * (inv_temp * grad_scale) * valid_mask).astype(
        jnp.bfloat16
    )
    return (slot_loss, gradients)


def slot_body(samples, weight, matches, positives):
    row_count, feat_width = samples.shape
    groups = lax.axis_size("label")
    local_count = weight.shape[1]
    label_count = weight.shape[2]
    clusters = groups * local_count
    pick_count = matches.shape[1]
    capacity = 2 * row_count * pick_count // clusters
    slot_ids, slot_row, slot_label = slot_tables(matches, positives, clusters, capacity)
    outgoing = samples[slot_row].reshape(clusters, capacity, feat_width)
    incoming, labels = (
        lax.all_to_all(outgoing, "label", split_axis=0, concat_axis=0, tiled=True),
        lax.all_to_all(slot_label, "label", split_axis=0, concat_axis=0, tiled=True),
    )
    incoming = incoming.reshape(groups, local_count, capacity, feat_width)
    labels = labels.reshape(groups, local_count, capacity)
    scores = jnp.einsum(
        "scpd,dcl->scpl",
        incoming,
        lax.all_gather(weight, "dp", axis=0, tiled=True),
        preferred_element_type=jnp.float32,
    )
    slot_loss, gradients = slot_terms(scores, labels)
    weight_grad = lax.psum_scatter(
        jnp.einsum("scpd,scpl->dcl", incoming, gradients, preferred_element_type=jnp.float32),
        "dp",
        scatter_dimension=0,
        tiled=True,
    ).astype(jnp.bfloat16)
    returned = lax.all_to_all(
        slot_loss.reshape(clusters, -1), "label", split_axis=0, concat_axis=0, tiled=True
    )
    per_match = returned.reshape(-1)[slot_ids].reshape(row_count, pick_count)
    sample_loss = jnp.sum(per_match, axis=1) / (pick_count * label_count)
    return (weight_grad, sample_loss)


def pack_kernel(parts, samples_ref, matches_ref, positives_ref, next_ref, *outs):
    next_ref[0] = 0
    rows, feat_width = samples_ref.shape
    part = rows // parts
    cluster = lax.broadcasted_iota(jnp.int32, (lanes, rows), 0)
    code = jnp.zeros((lanes, rows), jnp.int32)
    for pick in range(matches_ref.shape[0]):
        hit = cluster == matches_ref[pick : pick + 1]
        code = code + jnp.where(hit, positives_ref[pick : pick + 1] + 1, 0)
    code = code.astype(jnp.float32).T.astype(jnp.bfloat16)
    for place, out in enumerate(outs):
        span = slice(place * part, (place + 1) * part)
        out[:, :feat_width] = samples_ref[span]
        out[:, feat_width:] = code[span]


def pack_call(samples, matches, positives, parts):
    rows, feat_width = samples.shape
    whole = pl.BlockSpec(memory_space=pltpu.VMEM)
    block = jax.ShapeDtypeStruct((rows // parts, feat_width + lanes), jnp.bfloat16)
    return pl.pallas_call(
        functools.partial(pack_kernel, parts),
        out_shape=(jax.ShapeDtypeStruct((1,), jnp.int32),) + (block,) * parts,
        in_specs=[whole, whole, whole],
        out_specs=(pl.BlockSpec(memory_space=pltpu.SMEM),) + (whole,) * parts,
        compiler_params=pltpu.CompilerParams(vmem_limit_bytes=8 << 20),
        name="pack",
    )(samples, matches.T, positives.T)


def load(sources, targets, sems):
    copies = [
        pltpu.make_async_copy(source, target, sems.at[place])
        for place, (source, target) in enumerate(zip(sources, targets, strict=True))
    ]
    for copy in copies:
        copy.start()
    return copies


def row_scores(me, xs, ws, copies, places, depth):
    scores = None
    for w, copy, (offset, first) in zip(ws, copies, places, strict=True):
        if copy is not None:
            copy.wait()
        start = pl.multiple_of((me ^ offset) * depth + first, w.shape[0])
        rows = jnp.concatenate([x[:, pl.ds(start, w.shape[0])] for x in xs], axis=0)
        part = jnp.dot(rows, w[...], preferred_element_type=jnp.float32)
        scores = part if scores is None else scores + part
    return scores


def row_terms(scores, xs, label, local_count, grad_ref, loss_ref, at):
    feat_width = xs[0].shape[1] - lanes
    codes = jnp.concatenate([x[:, feat_width:] for x in xs], axis=0).astype(jnp.float32)
    count = codes.shape[0]
    lane = lax.broadcasted_iota(jnp.int32, codes.shape, 1)
    label_count = scores.shape[1] // local_count
    label_ids = lax.broadcasted_iota(jnp.int32, (count, label_count), 1) + 1
    label_ids = label_ids.astype(jnp.float32)
    loss = None
    for cluster in range(local_count):
        span = slice(cluster * label_count, (cluster + 1) * label_count)
        mine = lane == label * local_count + cluster
        code = jnp.sum(jnp.where(mine, codes, 0.0), axis=1, keepdims=True)
        logits = scores[:, span] * inv_temp
        hit = label_ids == code
        decay = jnp.exp(-jnp.abs(logits))
        each = jnp.maximum(logits, 0.0) + jnp.log1p(decay) - jnp.where(hit, logits, 0.0)
        share = jnp.where(logits >= 0.0, 1.0, decay) / (1.0 + decay)
        valid = code > 0.0
        grad = (share - jnp.where(hit, 1.0, 0.0)) * (inv_temp * grad_scale)
        grad_ref[span, at : at + count] = jnp.where(valid, grad, 0.0).T.astype(jnp.bfloat16)
        sums = jnp.where(valid, jnp.sum(each, axis=1, keepdims=True), 0.0)
        loss = sums if loss is None else loss + sums
    loss_ref[:, at : at + count] = jnp.broadcast_to(loss, (count, lanes)).T[0:1]


def stage_kernel(groups, places, depth, local_count, offsets, adds, *refs):
    take = iter(refs)

    def some(count):
        return [next(take) for _ in range(count)]

    (where_ref,) = some(1)
    ins = some(sum(groups) + len(places) + adds)
    next_ref, grad_ref, loss_ref = some(3)
    outs = some(len(offsets) * (local_count if adds else 1))
    xs, ws, sums = some(sum(groups)), some(len(places)), some(adds)
    (sems,), totals = some(1), some(1 - adds)
    me, label = where_ref[0], where_ref[1]
    next_ref[0] = me
    next_ref[1] = label
    copies = load(ins, xs + ws + sums, sems)
    weight_copies = copies[len(xs) : len(xs) + len(ws)]
    first, at = 0, 0
    for size in groups:
        for copy in copies[first : first + size]:
            copy.wait()
        group = xs[first : first + size]
        scores = row_scores(me, group, ws, weight_copies, places, depth)
        weight_copies = [None] * len(ws)
        row_terms(scores, group, label, local_count, grad_ref, loss_ref, at)
        first, at = first + size, at + scores.shape[0]
    for copy in copies[len(xs) + len(ws) :]:
        copy.wait()
    grads = grad_ref[...]
    tile = 256
    for place, offset in enumerate(offsets):
        for step in range(depth // tile):
            start = pl.multiple_of((me ^ offset) * depth + step * tile, tile)
            span = slice(step * tile, (step + 1) * tile)
            rows = jnp.concatenate([x[:, pl.ds(start, tile)] for x in xs], axis=0)
            total = jnp.dot(grads, rows, preferred_element_type=jnp.float32)
            if not adds:
                totals[0][place, :, span] = total
                continue
            total = total + sums[0][:, span]
            width = total.shape[0] // local_count
            for cluster in range(local_count):
                part = total[cluster * width : (cluster + 1) * width]
                outs[place * local_count + cluster][:, span] = part.astype(jnp.bfloat16)
        if not adds:
            pltpu.make_async_copy(totals[0].at[place], outs[place], sems.at[place]).start()
    if not adds:
        for place, out in enumerate(outs):
            pltpu.make_async_copy(totals[0].at[place], out, sems.at[place]).wait()


any_space = pl.BlockSpec(memory_space=pl.ANY)
whole = pl.BlockSpec(memory_space=pltpu.VMEM)
scalar = pl.BlockSpec(memory_space=pltpu.SMEM)


def stage_call(where, groups, ws, places, local_count, offsets, sums=()):
    xs = [x for group in groups for x in group]
    rows = sum(x.shape[0] for x in xs)
    feat_width = xs[0].shape[1] - lanes
    depth, columns = ws[0].shape
    inputs = [*xs, *ws, *sums]
    scratch = [pltpu.VMEM(array.shape, array.dtype) for array in inputs]
    scratch.append(pltpu.SemaphoreType.DMA((len(inputs),)))
    if sums:
        part = jax.ShapeDtypeStruct((columns // local_count, depth), jnp.bfloat16)
        outs = [part] * (local_count * len(offsets))
    else:
        outs = [jax.ShapeDtypeStruct((columns, depth), jnp.float32)] * len(offsets)
        scratch.append(pltpu.VMEM((len(offsets), columns, depth), jnp.float32))
    return pl.pallas_call(
        functools.partial(
            stage_kernel,
            tuple(len(group) for group in groups),
            places,
            depth,
            local_count,
            offsets,
            len(sums),
        ),
        out_shape=(
            jax.ShapeDtypeStruct((2,), jnp.int32),
            jax.ShapeDtypeStruct((columns, rows), jnp.bfloat16),
            jax.ShapeDtypeStruct((1, rows), jnp.float32),
            *outs,
        ),
        in_specs=[scalar] + [any_space] * len(inputs),
        out_specs=(scalar, whole, whole) + ((whole,) if sums else (any_space,)) * len(outs),
        scratch_shapes=scratch,
        compiler_params=pltpu.CompilerParams(vmem_limit_bytes=kernel_vmem),
        cost_estimate=pl.CostEstimate(
            flops=2 * rows * columns * (feat_width + depth * len(offsets)),
            bytes_accessed=2 * (rows + columns) * feat_width + 4 * columns * depth * len(offsets),
            transcendentals=2 * rows * columns,
        ),
        name="stage",
    )(where, *inputs)


def part_kernel(offset, lows, blocks, parts, gots, *refs):
    where_ref, refs = refs[0], refs[1:]
    xs_in, gs_in, refs = refs[:blocks], refs[blocks : blocks + parts], refs[blocks + parts :]
    sums_in, gots_in, refs = refs[0], refs[1 : 1 + gots], refs[1 + gots :]
    next_ref, out_ref, held, gs, sums = refs[:5]
    got, sems = refs[5], refs[-1]
    next_ref[0] = where_ref[0]
    next_ref[1] = where_ref[1]
    width, depth = out_ref.shape
    begin = pl.multiple_of((where_ref[0] ^ offset) * depth, depth)
    sources = [x.at[:, pl.ds(begin, depth)] for x in xs_in]
    targets, at = [], 0
    for x in xs_in:
        targets.append(held.at[pl.ds(at, x.shape[0])])
        at += x.shape[0]
    at = 0
    for g in gs_in:
        sources.append(g.at[pl.ds(lows, width)])
        targets.append(gs.at[:, pl.ds(at, g.shape[1])])
        at += g.shape[1]
    sources.append(sums_in.at[pl.ds(lows, width)])
    targets.append(sums)
    if gots_in:
        sources.append(gots_in[0])
        targets.append(got)
    for copy in load(sources, targets, sems):
        copy.wait()
    tile = 256
    for step in range(depth // tile):
        span = slice(step * tile, (step + 1) * tile)
        total = jnp.dot(gs[...], held[:, span], preferred_element_type=jnp.float32)
        total = total + sums[:, span]
        if gots_in:
            total = total + got[:, span].astype(jnp.float32)
        out_ref[:, span] = total.astype(out_ref.dtype)


def part_call(where, offset, lows, width, kind, xs, gs, sums, got=()):
    rows = sum(x.shape[0] for x in xs)
    depth = sums.shape[1]
    count = len(xs) + len(gs) + 1 + len(got)
    return pl.pallas_call(
        functools.partial(part_kernel, offset, lows, len(xs), len(gs), len(got)),
        out_shape=(
            jax.ShapeDtypeStruct((2,), jnp.int32),
            jax.ShapeDtypeStruct((width, depth), kind),
        ),
        in_specs=[scalar] + [any_space] * count,
        out_specs=(scalar, whole),
        scratch_shapes=[
            pltpu.VMEM((rows, depth), jnp.bfloat16),
            pltpu.VMEM((width, rows), jnp.bfloat16),
            pltpu.VMEM((width, depth), jnp.float32),
            *(pltpu.VMEM((width, depth), jnp.bfloat16) for _ in got),
            pltpu.SemaphoreType.DMA((count,)),
        ],
        compiler_params=pltpu.CompilerParams(vmem_limit_bytes=kernel_vmem),
        cost_estimate=pl.CostEstimate(
            flops=2 * rows * depth * width,
            bytes_accessed=2 * rows * depth + 6 * depth * width,
            transcendentals=0,
        ),
        name="part",
    )(where, *xs, *gs, sums, *got)


def after(value, *earlier):
    return lax.optimization_barrier((value, earlier))[0]


def ring_body(samples, weight, matches, positives):
    row_count, feat_width = samples.shape
    depth, local_count, label_count = weight.shape
    groups = lax.axis_size("label")
    pick_count = matches.shape[1]
    clusters = groups * local_count
    dp = lax.axis_index("dp")
    label = lax.axis_index("label")
    where = jnp.stack([dp, label]).astype(jnp.int32)

    chips = groups // 2
    hop = [(z * 2 + c, ring_next[z] * 2 + c) for z in range(chips) for c in range(2)]
    swap = [(i, i ^ 1) for i in range(groups)]
    along_x = [(i, i ^ 1) for i in range(4)]
    along_y = [(i, i ^ 2) for i in range(4)]

    packed, block = pack_call(samples, matches, positives, 1)
    flat = after(weight.reshape(depth, local_count * label_count), packed)
    half = depth // 2
    mine = [block]
    mine.append(lax.ppermute(block, "label", hop))
    w_x = lax.ppermute(flat, "dp", along_x)
    w_y = lax.ppermute(flat, "dp", along_y)
    mine[1] = after(mine[1], w_x, w_y)
    mine.append(lax.ppermute(mine[1], "label", hop))
    far_x = lax.ppermute(w_x[:half], "dp", along_y)
    far_y = lax.ppermute(w_y[half:], "dp", along_x)
    mine[2] = after(mine[2], far_x, far_y)
    ws = [flat, w_x, w_y, far_x, far_y]
    places = ((0, 0), (1, 0), (2, 0), (3, 0), (3, half))
    early = [[block, lax.ppermute(block, "label", swap)] for block in mine]

    offsets = (3, 1, 2, 0)
    last = lax.ppermute(mine[-1], "label", hop)
    token, _, loss, *sums = stage_call(where, early, ws, places, local_count, offsets)
    last = after(last, token)
    losses = [loss]
    sums = dict(zip(offsets, sums))

    low, full = jnp.bfloat16, jnp.float32
    xs = [last, lax.ppermute(last, "label", swap)]
    token, grads, loss, far_0, far_1 = stage_call(
        token, [xs], ws, places, local_count, (3,), (sums[3],)
    )
    losses.append(loss)
    far_x = lax.ppermute(far_0, "dp", along_x)
    far_y = lax.ppermute(far_1, "dp", along_y)
    gs = [grads]
    order = []
    for z in range(chips):
        for c in range(2):
            at, rows = z, []
            for _ in range(chips):
                rows.append([at * 2 + c, at * 2 + 1 - c])
                at = ring_prev[at]
            order.append(rows)
    order = jnp.array(order, jnp.int32)[label]

    width = label_count
    token, near_x = part_call(token, 1, 0, width, low, xs, gs, sums[1])
    got_x = lax.ppermute(near_x, "dp", along_x)
    token, near_y = part_call(token, 2, width, width, low, xs, gs, sums[2])
    got_y = lax.ppermute(near_y, "dp", along_y)
    token, own = part_call(token, 0, 0, 2 * width, full, xs, gs, sums[0])
    token, on_y = part_call(token, 2, 0, width, low, xs, gs, sums[2], (far_x,))
    pass_y = lax.ppermute(on_y, "dp", along_y)
    token, on_x = part_call(token, 1, width, width, low, xs, gs, sums[1], (far_y,))
    pass_x = lax.ppermute(on_x, "dp", along_x)
    by_step = after(jnp.concatenate(losses, axis=1).reshape(groups, row_count), token)
    total = jnp.zeros((groups, row_count), jnp.float32)
    total = total.at[order.reshape(-1)].set(by_step)
    returned = lax.all_to_all(total, "label", split_axis=0, concat_axis=0, tiled=True)
    sample_loss = jnp.sum(returned, axis=0) / (pick_count * label_count)

    first = own[:width] + got_x.astype(jnp.float32) + pass_y.astype(jnp.float32)
    second = own[width:] + got_y.astype(jnp.float32) + pass_x.astype(jnp.float32)
    weight_grad = jnp.transpose(jnp.stack([first, second]), (2, 0, 1)).astype(jnp.bfloat16)
    return (weight_grad, sample_loss)


def body(samples, weight, matches, positives):
    if (lax.axis_size("dp"), lax.axis_size("label"), weight.shape[1]) == (4, 8, 2):
        return ring_body(samples, weight, matches, positives)
    return slot_body(samples, weight, matches, positives)


def solution(mesh):
    placed = (
        P(("dp", "label"), None),
        P("dp", "label", None),
        P(("dp", "label"), None),
        P(("dp", "label"), None),
    )
    return jax.shard_map(
        body,
        mesh=mesh,
        in_specs=placed,
        out_specs=(P("dp", "label", None), P(("dp", "label"))),
        check_vma=False,
    )
```

```python
import functools

import jax
import jax.numpy as jnp
from jax import lax
from jax.experimental import pallas as pl
from jax.experimental.pallas import tpu as pltpu
from jax.sharding import PartitionSpec as P

inv_temp = 2.0
grad_scale = 0.03125

ring_next = (1, 3, 0, 2)
ring_prev = (2, 0, 3, 1)
halves = 2
kernel_vmem = 32 << 20
lanes = 128


def slot_tables(matches, positives, clusters, capacity):
    row_count, pick_count = matches.shape
    flat_ids = matches.reshape(row_count * pick_count)
    onehot = (flat_ids[:, None] == jnp.arange(clusters, dtype=jnp.int32)[None, :]).astype(jnp.int32)
    rank_ids = jnp.sum((jnp.cumsum(onehot, axis=0) - 1) * onehot, axis=1)
    slot_ids = flat_ids * capacity + rank_ids
    owners = jnp.arange(row_count * pick_count, dtype=jnp.int32) // pick_count
    slot_row = jnp.zeros((clusters * capacity,), jnp.int32).at[slot_ids].set(owners)
    slot_label = (
        jnp.full((clusters * capacity,), -1, jnp.int32)
        .at[slot_ids]
        .set(positives.reshape(row_count * pick_count))
    )
    return (slot_ids, slot_row, slot_label.reshape(clusters, capacity))


def slot_terms(scores, labels):
    logits = scores * inv_temp
    label_ids = jnp.arange(scores.shape[-1], dtype=jnp.int32)
    targets = (label_ids == labels[..., None]).astype(jnp.float32)
    valid_mask = (labels >= 0).astype(jnp.float32)[..., None]
    per_label = jnp.maximum(logits, 0.0) + jnp.log1p(jnp.exp(-jnp.abs(logits))) - targets * logits
    slot_loss = jnp.sum(per_label * valid_mask, axis=-1)
    gradients = ((jax.nn.sigmoid(logits) - targets) * (inv_temp * grad_scale) * valid_mask).astype(
        jnp.bfloat16
    )
    return (slot_loss, gradients)


def slot_body(samples, weight, matches, positives):
    row_count, feat_width = samples.shape
    groups = lax.axis_size("label")
    local_count = weight.shape[1]
    label_count = weight.shape[2]
    clusters = groups * local_count
    pick_count = matches.shape[1]
    capacity = 2 * row_count * pick_count // clusters
    slot_ids, slot_row, slot_label = slot_tables(matches, positives, clusters, capacity)
    outgoing = samples[slot_row].reshape(clusters, capacity, feat_width)
    incoming, labels = (
        lax.all_to_all(outgoing, "label", split_axis=0, concat_axis=0, tiled=True),
        lax.all_to_all(slot_label, "label", split_axis=0, concat_axis=0, tiled=True),
    )
    incoming = incoming.reshape(groups, local_count, capacity, feat_width)
    labels = labels.reshape(groups, local_count, capacity)
    scores = jnp.einsum(
        "scpd,dcl->scpl",
        incoming,
        lax.all_gather(weight, "dp", axis=0, tiled=True),
        preferred_element_type=jnp.float32,
    )
    slot_loss, gradients = slot_terms(scores, labels)
    weight_grad = lax.psum_scatter(
        jnp.einsum("scpd,scpl->dcl", incoming, gradients, preferred_element_type=jnp.float32),
        "dp",
        scatter_dimension=0,
        tiled=True,
    ).astype(jnp.bfloat16)
    returned = lax.all_to_all(
        slot_loss.reshape(clusters, -1), "label", split_axis=0, concat_axis=0, tiled=True
    )
    per_match = returned.reshape(-1)[slot_ids].reshape(row_count, pick_count)
    sample_loss = jnp.sum(per_match, axis=1) / (pick_count * label_count)
    return (weight_grad, sample_loss)


def pack_kernel(parts, where_ref, samples_ref, matches_ref, positives_ref, next_ref, *outs):
    next_ref[0] = where_ref[0]
    next_ref[1] = where_ref[1]
    rows, feat_width = samples_ref.shape
    part = rows // parts
    cluster = lax.broadcasted_iota(jnp.int32, (lanes, rows), 0)
    code = jnp.zeros((lanes, rows), jnp.int32)
    for pick in range(matches_ref.shape[0]):
        hit = cluster == matches_ref[pick : pick + 1]
        code = code + jnp.where(hit, positives_ref[pick : pick + 1] + 1, 0)
    code = code.astype(jnp.float32).T.astype(jnp.bfloat16)
    for place, out in enumerate(outs):
        span = slice(place * part, (place + 1) * part)
        out[:, :feat_width] = samples_ref[span]
        out[:, feat_width:] = code[span]


def pack_call(where, samples, matches, positives, parts):
    rows, feat_width = samples.shape
    block = jax.ShapeDtypeStruct((rows // parts, feat_width + lanes), jnp.bfloat16)
    return pl.pallas_call(
        functools.partial(pack_kernel, parts),
        out_shape=(jax.ShapeDtypeStruct((2,), jnp.int32),) + (block,) * parts,
        in_specs=[scalar, whole, whole, whole],
        out_specs=(scalar,) + (whole,) * parts,
        compiler_params=pltpu.CompilerParams(vmem_limit_bytes=8 << 20),
        name="pack",
    )(where, samples, matches.T, positives.T)


def load(sources, targets, sems):
    copies = [
        pltpu.make_async_copy(source, target, sems.at[place])
        for place, (source, target) in enumerate(zip(sources, targets, strict=True))
    ]
    for copy in copies:
        copy.start()
    return copies


def row_scores(me, xs, ws, copies, places, depth):
    scores = None
    for w, copy, (offset, first) in zip(ws, copies, places, strict=True):
        if copy is not None:
            copy.wait()
        start = pl.multiple_of((me ^ offset) * depth + first, w.shape[0])
        rows = jnp.concatenate([x[:, pl.ds(start, w.shape[0])] for x in xs], axis=0)
        part = jnp.dot(rows, w[...], preferred_element_type=jnp.float32)
        scores = part if scores is None else scores + part
    return scores


def row_terms(scores, xs, label, local_count, grad_ref, loss_ref, at):
    feat_width = xs[0].shape[1] - lanes
    codes = jnp.concatenate([x[:, feat_width:] for x in xs], axis=0).astype(jnp.float32)
    count = codes.shape[0]
    lane = lax.broadcasted_iota(jnp.int32, codes.shape, 1)
    label_count = scores.shape[1] // local_count
    label_ids = lax.broadcasted_iota(jnp.int32, (count, label_count), 1) + 1
    label_ids = label_ids.astype(jnp.float32)
    loss = None
    for cluster in range(local_count):
        span = slice(cluster * label_count, (cluster + 1) * label_count)
        mine = lane == label * local_count + cluster
        code = jnp.sum(jnp.where(mine, codes, 0.0), axis=1, keepdims=True)
        logits = scores[:, span] * inv_temp
        hit = label_ids == code
        decay = jnp.exp(-jnp.abs(logits))
        each = jnp.maximum(logits, 0.0) + jnp.log1p(decay) - jnp.where(hit, logits, 0.0)
        share = jnp.where(logits >= 0.0, 1.0, decay) / (1.0 + decay)
        valid = code > 0.0
        grad = (share - jnp.where(hit, 1.0, 0.0)) * (inv_temp * grad_scale)
        grad_ref[span, at : at + count] = jnp.where(valid, grad, 0.0).T.astype(jnp.bfloat16)
        sums = jnp.where(valid, jnp.sum(each, axis=1, keepdims=True), 0.0)
        loss = sums if loss is None else loss + sums
    loss_ref[:, at : at + count] = jnp.broadcast_to(loss, (count, lanes)).T[0:1]


def stage_kernel(groups, places, depth, local_count, offsets, adds, *refs):
    take = iter(refs)

    def some(count):
        return [next(take) for _ in range(count)]

    (where_ref,) = some(1)
    ins = some(sum(groups) + len(places) + adds)
    next_ref, grad_ref, loss_ref = some(3)
    outs = some(len(offsets) * (local_count if adds else 1))
    xs, ws, sums = some(sum(groups)), some(len(places)), some(adds)
    (sems,), totals = some(1), some(1 - adds)
    me, label = where_ref[0], where_ref[1]
    next_ref[0] = me
    next_ref[1] = label
    copies = load(ins, xs + ws + sums, sems)
    weight_copies = copies[len(xs) : len(xs) + len(ws)]
    first, at = 0, 0
    for size in groups:
        for copy in copies[first : first + size]:
            copy.wait()
        group = xs[first : first + size]
        scores = row_scores(me, group, ws, weight_copies, places, depth)
        weight_copies = [None] * len(ws)
        row_terms(scores, group, label, local_count, grad_ref, loss_ref, at)
        first, at = first + size, at + scores.shape[0]
    for copy in copies[len(xs) + len(ws) :]:
        copy.wait()
    grads = grad_ref[...]
    tile = 256
    for place, offset in enumerate(offsets):
        for step in range(depth // tile):
            start = pl.multiple_of((me ^ offset) * depth + step * tile, tile)
            span = slice(step * tile, (step + 1) * tile)
            rows = jnp.concatenate([x[:, pl.ds(start, tile)] for x in xs], axis=0)
            total = jnp.dot(grads, rows, preferred_element_type=jnp.float32)
            if not adds:
                totals[0][place, :, span] = total
                continue
            total = total + sums[0][:, span]
            width = total.shape[0] // local_count
            for cluster in range(local_count):
                part = total[cluster * width : (cluster + 1) * width]
                outs[place * local_count + cluster][:, span] = part.astype(jnp.bfloat16)
        if not adds:
            pltpu.make_async_copy(totals[0].at[place], outs[place], sems.at[place]).start()
    if not adds:
        for place, out in enumerate(outs):
            pltpu.make_async_copy(totals[0].at[place], out, sems.at[place]).wait()


any_space = pl.BlockSpec(memory_space=pl.ANY)
whole = pl.BlockSpec(memory_space=pltpu.VMEM)
scalar = pl.BlockSpec(memory_space=pltpu.SMEM)


def stage_call(where, groups, ws, places, local_count, offsets):
    xs = [x for group in groups for x in group]
    rows = sum(x.shape[0] for x in xs)
    feat_width = xs[0].shape[1] - lanes
    depth, columns = ws[0].shape
    sums = ()
    inputs = [*xs, *ws, *sums]
    scratch = [pltpu.VMEM(array.shape, array.dtype) for array in inputs]
    scratch.append(pltpu.SemaphoreType.DMA((len(inputs),)))
    if sums:
        part = jax.ShapeDtypeStruct((columns // local_count, depth), jnp.bfloat16)
        outs = [part] * (local_count * len(offsets))
    else:
        outs = [jax.ShapeDtypeStruct((columns, depth), jnp.float32)] * len(offsets)
        scratch.append(pltpu.VMEM((len(offsets), columns, depth), jnp.float32))
    return pl.pallas_call(
        functools.partial(
            stage_kernel,
            tuple(len(group) for group in groups),
            places,
            depth,
            local_count,
            offsets,
            len(sums),
        ),
        out_shape=(
            jax.ShapeDtypeStruct((2,), jnp.int32),
            jax.ShapeDtypeStruct((columns, rows), jnp.bfloat16),
            jax.ShapeDtypeStruct((1, rows), jnp.float32),
            *outs,
        ),
        in_specs=[scalar] + [any_space] * len(inputs),
        out_specs=(scalar, whole, whole) + ((whole,) if sums else (any_space,)) * len(outs),
        scratch_shapes=scratch,
        compiler_params=pltpu.CompilerParams(vmem_limit_bytes=kernel_vmem),
        cost_estimate=pl.CostEstimate(
            flops=2 * rows * columns * (feat_width + depth * len(offsets)),
            bytes_accessed=2 * (rows + columns) * feat_width + 4 * columns * depth * len(offsets),
            transcendentals=2 * rows * columns,
        ),
        name="stage",
    )(where, *inputs)


def grad_tiles(me, offset, xs, grads, sums, depth):
    tile = 256
    for step in range(depth // tile):
        start = pl.multiple_of((me ^ offset) * depth + step * tile, tile)
        span = slice(step * tile, (step + 1) * tile)
        rows = jnp.concatenate([x[:, pl.ds(start, tile)] for x in xs], axis=0)
        total = jnp.dot(grads, rows, preferred_element_type=jnp.float32)
        yield span, total + sums[:, span]


def last_kernel(blocks, places, depth, local_count, offset, where_ref, *refs):
    xs, ws, refs = refs[:blocks], refs[blocks : blocks + len(places)], refs[blocks + len(places) :]
    sums, next_ref, grad_ref, loss_ref, *outs = refs
    me, label = where_ref[0], where_ref[1]
    next_ref[0] = me
    next_ref[1] = label
    scores = row_scores(me, xs, ws, [None] * len(ws), places, depth)
    row_terms(scores, xs, label, local_count, grad_ref, loss_ref, 0)
    for span, total in grad_tiles(me, offset, xs, grad_ref[...], sums, depth):
        width = total.shape[0] // local_count
        for cluster, out in enumerate(outs):
            out[:, span] = total[cluster * width : (cluster + 1) * width].astype(out.dtype)


def last_call(where, xs, ws, places, local_count, offset, sums):
    rows = sum(x.shape[0] for x in xs)
    feat_width = xs[0].shape[1] - lanes
    depth, columns = ws[0].shape
    return pl.pallas_call(
        functools.partial(last_kernel, len(xs), places, depth, local_count, offset),
        out_shape=(
            jax.ShapeDtypeStruct((2,), jnp.int32),
            jax.ShapeDtypeStruct((columns, rows), jnp.bfloat16),
            jax.ShapeDtypeStruct((1, rows), jnp.float32),
        )
        + (jax.ShapeDtypeStruct((columns // local_count, depth), jnp.bfloat16),) * local_count,
        in_specs=[scalar] + [whole] * (len(xs) + len(ws) + 1),
        out_specs=(scalar,) + (whole,) * (2 + local_count),
        compiler_params=pltpu.CompilerParams(vmem_limit_bytes=16 << 20),
        cost_estimate=pl.CostEstimate(
            flops=2 * rows * columns * (feat_width + depth),
            bytes_accessed=2 * (rows + columns) * feat_width + 6 * columns * depth,
            transcendentals=2 * rows * columns,
        ),
        name="last",
    )(where, *xs, *ws, sums)


def near_kernel(blocks, where_ref, *refs):
    ins, (grads, next_ref, near_x, near_y, on_x, on_y, own) = refs[: blocks + 3], refs[
        blocks + 3 : blocks + 10
    ]
    held, sems = refs[blocks + 10 : -1], refs[-1]
    me = where_ref[0]
    next_ref[0] = me
    next_ref[1] = where_ref[1]
    copies = load(ins, held, sems)
    xs, sums = held[:blocks], held[blocks:]
    for copy in copies[: blocks + 1]:
        copy.wait()
    grads = grads[...]
    width, depth = near_x.shape
    for span, total in grad_tiles(me, 1, xs, grads, sums[0], depth):
        near_x[:, span] = total[:width].astype(near_x.dtype)
        on_x[:, span] = total[width:]
    copies[blocks + 1].wait()
    for span, total in grad_tiles(me, 2, xs, grads, sums[1], depth):
        on_y[:, span] = total[:width]
        near_y[:, span] = total[width:].astype(near_y.dtype)
    copies[blocks + 2].wait()
    for span, total in grad_tiles(me, 0, xs, grads, sums[2], depth):
        own[:, span] = total


def near_call(where, xs, grads, sums):
    columns, depth = sums[0].shape
    rows = grads.shape[1]
    half = (columns // 2, depth)
    inputs = (*xs, sums[1], sums[2], sums[0])
    return pl.pallas_call(
        functools.partial(near_kernel, len(xs)),
        out_shape=(
            jax.ShapeDtypeStruct((2,), jnp.int32),
            jax.ShapeDtypeStruct(half, jnp.bfloat16),
            jax.ShapeDtypeStruct(half, jnp.bfloat16),
            jax.ShapeDtypeStruct(half, jnp.float32),
            jax.ShapeDtypeStruct(half, jnp.float32),
            jax.ShapeDtypeStruct((columns, depth), jnp.float32),
        ),
        in_specs=[scalar] + [any_space] * len(inputs) + [whole],
        out_specs=(scalar,) + (whole,) * 5,
        scratch_shapes=[
            *(pltpu.VMEM(array.shape, array.dtype) for array in inputs),
            pltpu.SemaphoreType.DMA((len(inputs),)),
        ],
        compiler_params=pltpu.CompilerParams(vmem_limit_bytes=58 << 20),
        cost_estimate=pl.CostEstimate(
            flops=6 * rows * columns * depth,
            bytes_accessed=22 * columns * depth,
            transcendentals=0,
        ),
        name="near",
    )(where, *inputs, grads)


def join_kernel(on_x, far_y, on_y, far_x, out_x, out_y):
    out_x[...] = (on_x[...] + far_y[...].astype(jnp.float32)).astype(out_x.dtype)
    out_y[...] = (on_y[...] + far_x[...].astype(jnp.float32)).astype(out_y.dtype)


def join_call(on_x, far_y, on_y, far_x):
    part = jax.ShapeDtypeStruct(far_x.shape, far_x.dtype)
    return pl.pallas_call(
        join_kernel,
        out_shape=(part, part),
        in_specs=[whole] * 4,
        out_specs=(whole, whole),
        compiler_params=pltpu.CompilerParams(vmem_limit_bytes=16 << 20),
        name="join",
    )(on_x, far_y, on_y, far_x)


def tie(*values):
    return lax.optimization_barrier(values)


def ring_body(samples, weight, matches, positives):
    row_count, feat_width = samples.shape
    depth, local_count, label_count = weight.shape
    groups = lax.axis_size("label")
    pick_count = matches.shape[1]
    clusters = groups * local_count
    dp = lax.axis_index("dp")
    label = lax.axis_index("label")
    where = jnp.stack([dp, label]).astype(jnp.int32)

    chips = groups // 2
    hop = [(z * 2 + c, ring_next[z] * 2 + c) for z in range(chips) for c in range(2)]
    swap = [(i, i ^ 1) for i in range(groups)]
    along_x = [(i, i ^ 1) for i in range(4)]
    along_y = [(i, i ^ 2) for i in range(4)]

    where, *blocks = pack_call(where, samples, matches, positives, halves)
    flat, where = tie(weight.reshape(depth, local_count * label_count), where)
    half = depth // 2

    def hops(blocks):
        return [lax.ppermute(block, "label", hop) for block in blocks]

    mine = [blocks, hops(blocks)]
    w_x = lax.ppermute(flat, "dp", along_x)
    w_y = lax.ppermute(flat, "dp", along_y)
    mine[1][-1], w_x, w_y = tie(mine[1][-1], w_x, w_y)
    mine.append(hops(mine[1]))
    far_x = lax.ppermute(w_x[:half], "dp", along_y)
    far_y = lax.ppermute(w_y[half:], "dp", along_x)
    mine[2][-1], far_x, far_y = tie(mine[2][-1], far_x, far_y)
    last = hops(mine[2])
    ws = [flat, w_x, w_y, far_x, far_y]
    places = ((0, 0), (1, 0), (2, 0), (3, 0), (3, half))

    def with_mates(blocks):
        return blocks + [lax.ppermute(block, "label", swap) for block in blocks]

    early = [with_mates(blocks) for blocks in mine]

    offsets = (3, 1, 2, 0)
    token, _, loss, *sums = stage_call(where, early, ws, places, local_count, offsets)
    token, *last = tie(token, *last)
    losses = [loss]
    sums = dict(zip(offsets, sums))

    xs = with_mates(last)
    token, grads, loss, far_0, far_1 = last_call(token, xs, ws, places, local_count, 3, sums[3])
    losses.append(loss)
    far_x = lax.ppermute(far_0, "dp", along_x)
    far_y = lax.ppermute(far_1, "dp", along_y)
    token, near_x, near_y, on_x, on_y, own = near_call(token, xs, grads, sums)
    got_x = lax.ppermute(near_x, "dp", along_x)
    got_y = lax.ppermute(near_y, "dp", along_y)
    on_x, on_y = join_call(on_x, far_y, on_y, far_x)
    width = label_count

    order = []
    for z in range(chips):
        for c in range(2):
            at, steps = z, []
            for _ in range(chips):
                steps.append([at * 2 + c, at * 2 + 1 - c])
                at = ring_prev[at]
            order.append(steps)
    order = jnp.array(order, jnp.int32)[label]
    by_step, on_x, on_y = tie(
        jnp.concatenate(losses, axis=1).reshape(groups, row_count), on_x, on_y
    )
    pass_x = lax.ppermute(on_x, "dp", along_x)
    pass_y = lax.ppermute(on_y, "dp", along_y)
    total = jnp.zeros((groups, row_count), jnp.float32)
    total = total.at[order.reshape(-1)].set(by_step)
    returned = lax.all_to_all(total, "label", split_axis=0, concat_axis=0, tiled=True)
    sample_loss = jnp.sum(returned, axis=0) / (pick_count * label_count)

    first = own[:width] + got_x.astype(jnp.float32) + pass_y.astype(jnp.float32)
    second = own[width:] + got_y.astype(jnp.float32) + pass_x.astype(jnp.float32)
    weight_grad = jnp.transpose(jnp.stack([first, second]), (2, 0, 1)).astype(jnp.bfloat16)
    return (weight_grad, sample_loss)


def body(samples, weight, matches, positives):
    if (lax.axis_size("dp"), lax.axis_size("label"), weight.shape[1]) == (4, 8, 2):
        return ring_body(samples, weight, matches, positives)
    return slot_body(samples, weight, matches, positives)


def solution(mesh):
    placed = (
        P(("dp", "label"), None),
        P("dp", "label", None),
        P(("dp", "label"), None),
        P(("dp", "label"), None),
    )
    return jax.shard_map(
        body,
        mesh=mesh,
        in_specs=placed,
        out_specs=(P("dp", "label", None), P(("dp", "label"))),
        check_vma=False,
    )
```

```python
import functools

import jax
import jax.numpy as jnp
from jax import lax
from jax.experimental import pallas as pl
from jax.experimental.pallas import tpu as pltpu
from jax.sharding import PartitionSpec as P

inv_temp = 2.0
grad_scale = 0.03125

ring_next = (1, 3, 0, 2)
ring_prev = (2, 0, 3, 1)
halves = 2
kernel_vmem = 32 << 20
lanes = 128


def slot_tables(matches, positives, clusters, capacity):
    row_count, pick_count = matches.shape
    flat_ids = matches.reshape(row_count * pick_count)
    onehot = (flat_ids[:, None] == jnp.arange(clusters, dtype=jnp.int32)[None, :]).astype(jnp.int32)
    rank_ids = jnp.sum((jnp.cumsum(onehot, axis=0) - 1) * onehot, axis=1)
    slot_ids = flat_ids * capacity + rank_ids
    owners = jnp.arange(row_count * pick_count, dtype=jnp.int32) // pick_count
    slot_row = jnp.zeros((clusters * capacity,), jnp.int32).at[slot_ids].set(owners)
    slot_label = (
        jnp.full((clusters * capacity,), -1, jnp.int32)
        .at[slot_ids]
        .set(positives.reshape(row_count * pick_count))
    )
    return (slot_ids, slot_row, slot_label.reshape(clusters, capacity))


def slot_terms(scores, labels):
    logits = scores * inv_temp
    label_ids = jnp.arange(scores.shape[-1], dtype=jnp.int32)
    targets = (label_ids == labels[..., None]).astype(jnp.float32)
    valid_mask = (labels >= 0).astype(jnp.float32)[..., None]
    per_label = jnp.maximum(logits, 0.0) + jnp.log1p(jnp.exp(-jnp.abs(logits))) - targets * logits
    slot_loss = jnp.sum(per_label * valid_mask, axis=-1)
    gradients = ((jax.nn.sigmoid(logits) - targets) * (inv_temp * grad_scale) * valid_mask).astype(
        jnp.bfloat16
    )
    return (slot_loss, gradients)


def slot_body(samples, weight, matches, positives):
    row_count, feat_width = samples.shape
    groups = lax.axis_size("label")
    local_count = weight.shape[1]
    label_count = weight.shape[2]
    clusters = groups * local_count
    pick_count = matches.shape[1]
    capacity = 2 * row_count * pick_count // clusters
    slot_ids, slot_row, slot_label = slot_tables(matches, positives, clusters, capacity)
    outgoing = samples[slot_row].reshape(clusters, capacity, feat_width)
    incoming, labels = (
        lax.all_to_all(outgoing, "label", split_axis=0, concat_axis=0, tiled=True),
        lax.all_to_all(slot_label, "label", split_axis=0, concat_axis=0, tiled=True),
    )
    incoming = incoming.reshape(groups, local_count, capacity, feat_width)
    labels = labels.reshape(groups, local_count, capacity)
    scores = jnp.einsum(
        "scpd,dcl->scpl",
        incoming,
        lax.all_gather(weight, "dp", axis=0, tiled=True),
        preferred_element_type=jnp.float32,
    )
    slot_loss, gradients = slot_terms(scores, labels)
    weight_grad = lax.psum_scatter(
        jnp.einsum("scpd,scpl->dcl", incoming, gradients, preferred_element_type=jnp.float32),
        "dp",
        scatter_dimension=0,
        tiled=True,
    ).astype(jnp.bfloat16)
    returned = lax.all_to_all(
        slot_loss.reshape(clusters, -1), "label", split_axis=0, concat_axis=0, tiled=True
    )
    per_match = returned.reshape(-1)[slot_ids].reshape(row_count, pick_count)
    sample_loss = jnp.sum(per_match, axis=1) / (pick_count * label_count)
    return (weight_grad, sample_loss)


def pack_kernel(parts, where_ref, samples_ref, matches_ref, positives_ref, next_ref, *outs):
    next_ref[0] = where_ref[0]
    next_ref[1] = where_ref[1]
    rows, feat_width = samples_ref.shape
    part = rows // parts
    cluster = lax.broadcasted_iota(jnp.int32, (lanes, rows), 0)
    code = jnp.zeros((lanes, rows), jnp.int32)
    for pick in range(matches_ref.shape[0]):
        hit = cluster == matches_ref[pick : pick + 1]
        code = code + jnp.where(hit, positives_ref[pick : pick + 1] + 1, 0)
    code = code.astype(jnp.float32).T.astype(jnp.bfloat16)
    for place, out in enumerate(outs):
        span = slice(place * part, (place + 1) * part)
        out[:, :feat_width] = samples_ref[span]
        out[:, feat_width:] = code[span]


def pack_call(where, samples, matches, positives, parts):
    rows, feat_width = samples.shape
    block = jax.ShapeDtypeStruct((rows // parts, feat_width + lanes), jnp.bfloat16)
    return pl.pallas_call(
        functools.partial(pack_kernel, parts),
        out_shape=(jax.ShapeDtypeStruct((2,), jnp.int32),) + (block,) * parts,
        in_specs=[scalar, whole, whole, whole],
        out_specs=(scalar,) + (whole,) * parts,
        compiler_params=pltpu.CompilerParams(vmem_limit_bytes=8 << 20),
        name="pack",
    )(where, samples, matches.T, positives.T)


def load(sources, targets, sems):
    copies = [
        pltpu.make_async_copy(source, target, sems.at[place])
        for place, (source, target) in enumerate(zip(sources, targets, strict=True))
    ]
    for copy in copies:
        copy.start()
    return copies


def row_scores(me, xs, ws, copies, places, depth):
    scores = None
    for w, copy, (offset, first) in zip(ws, copies, places, strict=True):
        if copy is not None:
            copy.wait()
        start = pl.multiple_of((me ^ offset) * depth + first, w.shape[0])
        rows = jnp.concatenate([x[:, pl.ds(start, w.shape[0])] for x in xs], axis=0)
        part = jnp.dot(rows, w[...], preferred_element_type=jnp.float32)
        scores = part if scores is None else scores + part
    return scores


def row_terms(scores, xs, label, local_count, grad_ref, loss_ref, at):
    feat_width = xs[0].shape[1] - lanes
    codes = jnp.concatenate([x[:, feat_width:] for x in xs], axis=0).astype(jnp.float32)
    count = codes.shape[0]
    lane = lax.broadcasted_iota(jnp.int32, codes.shape, 1)
    label_count = scores.shape[1] // local_count
    label_ids = lax.broadcasted_iota(jnp.int32, (count, label_count), 1) + 1
    label_ids = label_ids.astype(jnp.float32)
    loss = None
    for cluster in range(local_count):
        span = slice(cluster * label_count, (cluster + 1) * label_count)
        mine = lane == label * local_count + cluster
        code = jnp.sum(jnp.where(mine, codes, 0.0), axis=1, keepdims=True)
        logits = scores[:, span] * inv_temp
        hit = label_ids == code
        decay = jnp.exp(-jnp.abs(logits))
        each = jnp.maximum(logits, 0.0) + jnp.log1p(decay) - jnp.where(hit, logits, 0.0)
        share = jnp.where(logits >= 0.0, 1.0, decay) / (1.0 + decay)
        valid = code > 0.0
        grad = (share - jnp.where(hit, 1.0, 0.0)) * (inv_temp * grad_scale)
        grad_ref[span, at : at + count] = jnp.where(valid, grad, 0.0).T.astype(jnp.bfloat16)
        sums = jnp.where(valid, jnp.sum(each, axis=1, keepdims=True), 0.0)
        loss = sums if loss is None else loss + sums
    loss_ref[:, at : at + count] = jnp.broadcast_to(loss, (count, lanes)).T[0:1]


def stage_kernel(groups, places, depth, local_count, offsets, adds, *refs):
    take = iter(refs)

    def some(count):
        return [next(take) for _ in range(count)]

    (where_ref,) = some(1)
    ins = some(sum(groups) + len(places) + adds)
    next_ref, grad_ref, loss_ref = some(3)
    outs = some(len(offsets) * (local_count if adds else 1))
    xs, ws, sums = some(sum(groups)), some(len(places)), some(adds)
    (sems,), totals = some(1), some(1 - adds)
    me, label = where_ref[0], where_ref[1]
    next_ref[0] = me
    next_ref[1] = label
    copies = load(ins, xs + ws + sums, sems)
    weight_copies = copies[len(xs) : len(xs) + len(ws)]
    first, at = 0, 0
    for size in groups:
        for copy in copies[first : first + size]:
            copy.wait()
        group = xs[first : first + size]
        scores = row_scores(me, group, ws, weight_copies, places, depth)
        weight_copies = [None] * len(ws)
        row_terms(scores, group, label, local_count, grad_ref, loss_ref, at)
        first, at = first + size, at + scores.shape[0]
    for copy in copies[len(xs) + len(ws) :]:
        copy.wait()
    grads = grad_ref[...]
    tile = 256
    for place, offset in enumerate(offsets):
        for step in range(depth // tile):
            start = pl.multiple_of((me ^ offset) * depth + step * tile, tile)
            span = slice(step * tile, (step + 1) * tile)
            rows = jnp.concatenate([x[:, pl.ds(start, tile)] for x in xs], axis=0)
            total = jnp.dot(grads, rows, preferred_element_type=jnp.float32)
            if not adds:
                totals[0][place, :, span] = total
                continue
            total = total + sums[0][:, span]
            width = total.shape[0] // local_count
            for cluster in range(local_count):
                part = total[cluster * width : (cluster + 1) * width]
                outs[place * local_count + cluster][:, span] = part.astype(jnp.bfloat16)
        if not adds:
            pltpu.make_async_copy(totals[0].at[place], outs[place], sems.at[place]).start()
    if not adds:
        for place, out in enumerate(outs):
            pltpu.make_async_copy(totals[0].at[place], out, sems.at[place]).wait()


any_space = pl.BlockSpec(memory_space=pl.ANY)
whole = pl.BlockSpec(memory_space=pltpu.VMEM)
scalar = pl.BlockSpec(memory_space=pltpu.SMEM)


def stage_call(where, groups, ws, places, local_count, offsets):
    xs = [x for group in groups for x in group]
    rows = sum(x.shape[0] for x in xs)
    feat_width = xs[0].shape[1] - lanes
    depth, columns = ws[0].shape
    sums = ()
    inputs = [*xs, *ws, *sums]
    scratch = [pltpu.VMEM(array.shape, array.dtype) for array in inputs]
    scratch.append(pltpu.SemaphoreType.DMA((len(inputs),)))
    if sums:
        part = jax.ShapeDtypeStruct((columns // local_count, depth), jnp.bfloat16)
        outs = [part] * (local_count * len(offsets))
    else:
        outs = [jax.ShapeDtypeStruct((columns, depth), jnp.float32)] * len(offsets)
        scratch.append(pltpu.VMEM((len(offsets), columns, depth), jnp.float32))
    return pl.pallas_call(
        functools.partial(
            stage_kernel,
            tuple(len(group) for group in groups),
            places,
            depth,
            local_count,
            offsets,
            len(sums),
        ),
        out_shape=(
            jax.ShapeDtypeStruct((2,), jnp.int32),
            jax.ShapeDtypeStruct((columns, rows), jnp.bfloat16),
            jax.ShapeDtypeStruct((1, rows), jnp.float32),
            *outs,
        ),
        in_specs=[scalar] + [any_space] * len(inputs),
        out_specs=(scalar, whole, whole) + ((whole,) if sums else (any_space,)) * len(outs),
        scratch_shapes=scratch,
        compiler_params=pltpu.CompilerParams(vmem_limit_bytes=kernel_vmem),
        cost_estimate=pl.CostEstimate(
            flops=2 * rows * columns * (feat_width + depth * len(offsets)),
            bytes_accessed=2 * (rows + columns) * feat_width + 4 * columns * depth * len(offsets),
            transcendentals=2 * rows * columns,
        ),
        name="stage",
    )(where, *inputs)


def grad_tiles(me, offset, xs, grads, sums, depth):
    tile = 256
    for step in range(depth // tile):
        start = pl.multiple_of((me ^ offset) * depth + step * tile, tile)
        span = slice(step * tile, (step + 1) * tile)
        rows = jnp.concatenate([x[:, pl.ds(start, tile)] for x in xs], axis=0)
        total = jnp.dot(grads, rows, preferred_element_type=jnp.float32)
        yield span, total + sums[:, span]


def last_kernel(blocks, places, depth, local_count, offset, where_ref, *refs):
    xs, ws, refs = refs[:blocks], refs[blocks : blocks + len(places)], refs[blocks + len(places) :]
    sums, next_ref, grad_ref, loss_ref, *outs = refs
    me, label = where_ref[0], where_ref[1]
    next_ref[0] = me
    next_ref[1] = label
    scores = row_scores(me, xs, ws, [None] * len(ws), places, depth)
    row_terms(scores, xs, label, local_count, grad_ref, loss_ref, 0)
    for span, total in grad_tiles(me, offset, xs, grad_ref[...], sums, depth):
        width = total.shape[0] // local_count
        for cluster, out in enumerate(outs):
            out[:, span] = total[cluster * width : (cluster + 1) * width].astype(out.dtype)


def last_call(where, xs, ws, places, local_count, offset, sums):
    rows = sum(x.shape[0] for x in xs)
    feat_width = xs[0].shape[1] - lanes
    depth, columns = ws[0].shape
    return pl.pallas_call(
        functools.partial(last_kernel, len(xs), places, depth, local_count, offset),
        out_shape=(
            jax.ShapeDtypeStruct((2,), jnp.int32),
            jax.ShapeDtypeStruct((columns, rows), jnp.bfloat16),
            jax.ShapeDtypeStruct((1, rows), jnp.float32),
        )
        + (jax.ShapeDtypeStruct((columns // local_count, depth), jnp.bfloat16),) * local_count,
        in_specs=[scalar] + [whole] * (len(xs) + len(ws) + 1),
        out_specs=(scalar,) + (whole,) * (2 + local_count),
        compiler_params=pltpu.CompilerParams(vmem_limit_bytes=16 << 20),
        cost_estimate=pl.CostEstimate(
            flops=2 * rows * columns * (feat_width + depth),
            bytes_accessed=2 * (rows + columns) * feat_width + 6 * columns * depth,
            transcendentals=2 * rows * columns,
        ),
        name="last",
    )(where, *xs, *ws, sums)


def near_kernel(blocks, where_ref, *refs):
    ins, (grads, next_ref, near_x, near_y, on_x, on_y, own) = refs[: blocks + 3], refs[
        blocks + 3 : blocks + 10
    ]
    held, sems = refs[blocks + 10 : -1], refs[-1]
    me = where_ref[0]
    next_ref[0] = me
    next_ref[1] = where_ref[1]
    copies = load(ins, held, sems)
    xs, sums = held[:blocks], held[blocks:]
    for copy in copies[: blocks + 1]:
        copy.wait()
    grads = grads[...]
    width, depth = near_x.shape
    for span, total in grad_tiles(me, 1, xs, grads, sums[0], depth):
        near_x[:, span] = total[:width].astype(near_x.dtype)
        on_x[:, span] = total[width:]
    copies[blocks + 1].wait()
    for span, total in grad_tiles(me, 2, xs, grads, sums[1], depth):
        on_y[:, span] = total[:width]
        near_y[:, span] = total[width:].astype(near_y.dtype)
    copies[blocks + 2].wait()
    for span, total in grad_tiles(me, 0, xs, grads, sums[2], depth):
        own[:, span] = total


def near_call(where, xs, grads, sums):
    columns, depth = sums[0].shape
    rows = grads.shape[1]
    half = (columns // 2, depth)
    inputs = (*xs, sums[1], sums[2], sums[0])
    return pl.pallas_call(
        functools.partial(near_kernel, len(xs)),
        out_shape=(
            jax.ShapeDtypeStruct((2,), jnp.int32),
            jax.ShapeDtypeStruct(half, jnp.bfloat16),
            jax.ShapeDtypeStruct(half, jnp.bfloat16),
            jax.ShapeDtypeStruct(half, jnp.float32),
            jax.ShapeDtypeStruct(half, jnp.float32),
            jax.ShapeDtypeStruct((columns, depth), jnp.float32),
        ),
        in_specs=[scalar] + [any_space] * len(inputs) + [whole],
        out_specs=(scalar,) + (whole,) * 5,
        scratch_shapes=[
            *(pltpu.VMEM(array.shape, array.dtype) for array in inputs),
            pltpu.SemaphoreType.DMA((len(inputs),)),
        ],
        compiler_params=pltpu.CompilerParams(vmem_limit_bytes=24 << 20),
        cost_estimate=pl.CostEstimate(
            flops=6 * rows * columns * depth,
            bytes_accessed=22 * columns * depth,
            transcendentals=0,
        ),
        name="near",
    )(where, *inputs, grads)


def join_kernel(on_x, far_y, on_y, far_x, out_x, out_y):
    out_x[...] = (on_x[...] + far_y[...].astype(jnp.float32)).astype(out_x.dtype)
    out_y[...] = (on_y[...] + far_x[...].astype(jnp.float32)).astype(out_y.dtype)


def join_call(on_x, far_y, on_y, far_x):
    part = jax.ShapeDtypeStruct(far_x.shape, far_x.dtype)
    return pl.pallas_call(
        join_kernel,
        out_shape=(part, part),
        in_specs=[whole] * 4,
        out_specs=(whole, whole),
        compiler_params=pltpu.CompilerParams(vmem_limit_bytes=4 << 20),
        name="join",
    )(on_x, far_y, on_y, far_x)


def base_kernel(own, got_x, got_y, out):
    width = got_x.shape[0]
    out[:width] = own[:width] + got_x[...].astype(jnp.float32)
    out[width:] = own[width:] + got_y[...].astype(jnp.float32)


def base_call(own, got_x, got_y):
    return pl.pallas_call(
        base_kernel,
        out_shape=jax.ShapeDtypeStruct(own.shape, own.dtype),
        in_specs=[whole] * 3,
        out_specs=whole,
        compiler_params=pltpu.CompilerParams(vmem_limit_bytes=4 << 20),
        name="base",
    )(own, got_x, got_y)


def final_kernel(base, pass_y, pass_x, out):
    tile = 256
    width = pass_y.shape[0]
    for step in range(out.shape[0] // tile):
        span = slice(step * tile, (step + 1) * tile)
        first = base[:width, span] + pass_y[:, span].astype(jnp.float32)
        second = base[width:, span] + pass_x[:, span].astype(jnp.float32)
        out[span, :width] = first.T.astype(out.dtype)
        out[span, width:] = second.T.astype(out.dtype)


def final_call(base, pass_y, pass_x):
    columns, depth = base.shape
    return pl.pallas_call(
        final_kernel,
        out_shape=jax.ShapeDtypeStruct((depth, columns), jnp.bfloat16),
        in_specs=[whole] * 3,
        out_specs=whole,
        compiler_params=pltpu.CompilerParams(vmem_limit_bytes=4 << 20),
        name="final",
    )(base, pass_y, pass_x)


def tie(*values):
    return lax.optimization_barrier(values)


def ring_body(samples, weight, matches, positives):
    row_count, feat_width = samples.shape
    depth, local_count, label_count = weight.shape
    groups = lax.axis_size("label")
    pick_count = matches.shape[1]
    clusters = groups * local_count
    dp = lax.axis_index("dp")
    label = lax.axis_index("label")
    where = jnp.stack([dp, label]).astype(jnp.int32)

    chips = groups // 2
    hop = [(z * 2 + c, ring_next[z] * 2 + c) for z in range(chips) for c in range(2)]
    swap = [(i, i ^ 1) for i in range(groups)]
    along_x = [(i, i ^ 1) for i in range(4)]
    along_y = [(i, i ^ 2) for i in range(4)]

    where, *blocks = pack_call(where, samples, matches, positives, halves)
    flat, where = tie(weight.reshape(depth, local_count * label_count), where)
    half = depth // 2

    def hops(blocks):
        return [lax.ppermute(block, "label", hop) for block in blocks]

    mine = [blocks, hops(blocks)]
    w_x = lax.ppermute(flat, "dp", along_x)
    w_y = lax.ppermute(flat, "dp", along_y)
    mine[1][-1], w_x, w_y = tie(mine[1][-1], w_x, w_y)
    mine.append(hops(mine[1]))
    far_x = lax.ppermute(w_x[:half], "dp", along_y)
    far_y = lax.ppermute(w_y[half:], "dp", along_x)
    mine[2][-1], far_x, far_y = tie(mine[2][-1], far_x, far_y)
    last = hops(mine[2])
    ws = [flat, w_x, w_y, far_x, far_y]
    places = ((0, 0), (1, 0), (2, 0), (3, 0), (3, half))

    def with_mates(blocks):
        return blocks + [lax.ppermute(block, "label", swap) for block in blocks]

    early = [with_mates(blocks) for blocks in mine]

    offsets = (3, 1, 2, 0)
    token, _, loss, *sums = stage_call(where, early, ws, places, local_count, offsets)
    token, *last = tie(token, *last)
    losses = [loss]
    sums = dict(zip(offsets, sums))

    xs = with_mates(last)
    token, grads, loss, far_0, far_1 = last_call(token, xs, ws, places, local_count, 3, sums[3])
    losses.append(loss)
    far_x = lax.ppermute(far_0, "dp", along_x)
    far_y = lax.ppermute(far_1, "dp", along_y)
    token, near_x, near_y, on_x, on_y, own = near_call(token, xs, grads, sums)
    got_x = lax.ppermute(near_x, "dp", along_x)
    got_y = lax.ppermute(near_y, "dp", along_y)
    on_x, on_y = join_call(on_x, far_y, on_y, far_x)

    order = []
    for z in range(chips):
        for c in range(2):
            at, steps = z, []
            for _ in range(chips):
                steps.append([at * 2 + c, at * 2 + 1 - c])
                at = ring_prev[at]
            order.append(steps)
    order = jnp.array(order, jnp.int32)[label]
    by_step, on_x, on_y = tie(
        jnp.concatenate(losses, axis=1).reshape(groups, row_count), on_x, on_y
    )
    pass_x = lax.ppermute(on_x, "dp", along_x)
    pass_y = lax.ppermute(on_y, "dp", along_y)
    total = jnp.zeros((groups, row_count), jnp.float32)
    total = total.at[order.reshape(-1)].set(by_step)
    returned = lax.all_to_all(total, "label", split_axis=0, concat_axis=0, tiled=True)
    sample_loss = jnp.sum(returned, axis=0) / (pick_count * label_count)

    weight_grad = final_call(base_call(own, got_x, got_y), pass_y, pass_x)
    weight_grad = weight_grad.reshape(depth, local_count, label_count)
    return (weight_grad, sample_loss)


def body(samples, weight, matches, positives):
    if (lax.axis_size("dp"), lax.axis_size("label"), weight.shape[1]) == (4, 8, 2):
        return ring_body(samples, weight, matches, positives)
    return slot_body(samples, weight, matches, positives)


def solution(mesh):
    placed = (
        P(("dp", "label"), None),
        P("dp", "label", None),
        P(("dp", "label"), None),
        P(("dp", "label"), None),
    )
    return jax.shard_map(
        body,
        mesh=mesh,
        in_specs=placed,
        out_specs=(P("dp", "label", None), P(("dp", "label"))),
        check_vma=False,
    )
```

```python
import functools

import jax
import jax.numpy as jnp
from jax import lax
from jax.experimental import pallas as pl
from jax.experimental.pallas import tpu as pltpu
from jax.sharding import PartitionSpec as P

inv_temp = 2.0
grad_scale = 0.03125

ring_next = (1, 3, 0, 2)
ring_prev = (2, 0, 3, 1)
halves = 2
kernel_vmem = 32 << 20
lanes = 128


def slot_tables(matches, positives, clusters, capacity):
    row_count, pick_count = matches.shape
    flat_ids = matches.reshape(row_count * pick_count)
    onehot = (flat_ids[:, None] == jnp.arange(clusters, dtype=jnp.int32)[None, :]).astype(jnp.int32)
    rank_ids = jnp.sum((jnp.cumsum(onehot, axis=0) - 1) * onehot, axis=1)
    slot_ids = flat_ids * capacity + rank_ids
    owners = jnp.arange(row_count * pick_count, dtype=jnp.int32) // pick_count
    slot_row = jnp.zeros((clusters * capacity,), jnp.int32).at[slot_ids].set(owners)
    slot_label = (
        jnp.full((clusters * capacity,), -1, jnp.int32)
        .at[slot_ids]
        .set(positives.reshape(row_count * pick_count))
    )
    return (slot_ids, slot_row, slot_label.reshape(clusters, capacity))


def slot_terms(scores, labels):
    logits = scores * inv_temp
    label_ids = jnp.arange(scores.shape[-1], dtype=jnp.int32)
    targets = (label_ids == labels[..., None]).astype(jnp.float32)
    valid_mask = (labels >= 0).astype(jnp.float32)[..., None]
    per_label = jnp.maximum(logits, 0.0) + jnp.log1p(jnp.exp(-jnp.abs(logits))) - targets * logits
    slot_loss = jnp.sum(per_label * valid_mask, axis=-1)
    gradients = ((jax.nn.sigmoid(logits) - targets) * (inv_temp * grad_scale) * valid_mask).astype(
        jnp.bfloat16
    )
    return (slot_loss, gradients)


def slot_body(samples, weight, matches, positives):
    row_count, feat_width = samples.shape
    groups = lax.axis_size("label")
    local_count = weight.shape[1]
    label_count = weight.shape[2]
    clusters = groups * local_count
    pick_count = matches.shape[1]
    capacity = 2 * row_count * pick_count // clusters
    slot_ids, slot_row, slot_label = slot_tables(matches, positives, clusters, capacity)
    outgoing = samples[slot_row].reshape(clusters, capacity, feat_width)
    incoming, labels = (
        lax.all_to_all(outgoing, "label", split_axis=0, concat_axis=0, tiled=True),
        lax.all_to_all(slot_label, "label", split_axis=0, concat_axis=0, tiled=True),
    )
    incoming = incoming.reshape(groups, local_count, capacity, feat_width)
    labels = labels.reshape(groups, local_count, capacity)
    scores = jnp.einsum(
        "scpd,dcl->scpl",
        incoming,
        lax.all_gather(weight, "dp", axis=0, tiled=True),
        preferred_element_type=jnp.float32,
    )
    slot_loss, gradients = slot_terms(scores, labels)
    weight_grad = lax.psum_scatter(
        jnp.einsum("scpd,scpl->dcl", incoming, gradients, preferred_element_type=jnp.float32),
        "dp",
        scatter_dimension=0,
        tiled=True,
    ).astype(jnp.bfloat16)
    returned = lax.all_to_all(
        slot_loss.reshape(clusters, -1), "label", split_axis=0, concat_axis=0, tiled=True
    )
    per_match = returned.reshape(-1)[slot_ids].reshape(row_count, pick_count)
    sample_loss = jnp.sum(per_match, axis=1) / (pick_count * label_count)
    return (weight_grad, sample_loss)


def pack_kernel(where_ref, samples_ref, matches_ref, positives_ref, next_ref, out):
    next_ref[0] = where_ref[0]
    next_ref[1] = where_ref[1]
    count, feat_width = samples_ref.shape
    half = lanes // 2
    cluster = lax.broadcasted_iota(jnp.int32, (half, 2 * count), 0)
    code = jnp.zeros((half, 2 * count), jnp.int32)
    for pick in range(matches_ref.shape[0]):
        hit = cluster == matches_ref[pick : pick + 1]
        code = code + jnp.where(hit, positives_ref[pick : pick + 1] + 1, 0)
    code = jnp.concatenate([code[:, :count], code[:, count:]], axis=0)
    out[:, :feat_width] = samples_ref[...]
    out[:, feat_width:] = code.astype(jnp.float32).T.astype(jnp.bfloat16)


def pack_call(where, samples, matches, positives):
    rows, feat_width = samples.shape
    block = jax.ShapeDtypeStruct((rows, feat_width + lanes), jnp.bfloat16)
    return pl.pallas_call(
        pack_kernel,
        out_shape=(jax.ShapeDtypeStruct((2,), jnp.int32),) + (block,),
        in_specs=[scalar, whole, whole, whole],
        out_specs=(scalar, whole),
        compiler_params=pltpu.CompilerParams(vmem_limit_bytes=8 << 20),
        name="pack",
    )(where, samples, matches.T, positives.T)


def load(sources, targets, sems):
    copies = [
        pltpu.make_async_copy(source, target, sems.at[place])
        for place, (source, target) in enumerate(zip(sources, targets, strict=True))
    ]
    for copy in copies:
        copy.start()
    return copies


def row_scores(me, xs, ws, copies, places, depth):
    scores = None
    for w, copy, (offset, first) in zip(ws, copies, places, strict=True):
        if copy is not None:
            copy.wait()
        start = pl.multiple_of((me ^ offset) * depth + first, w.shape[0])
        rows = jnp.concatenate([x[:, pl.ds(start, w.shape[0])] for x in xs], axis=0)
        part = jnp.dot(rows, w[...], preferred_element_type=jnp.float32)
        scores = part if scores is None else scores + part
    return scores


def row_terms(scores, xs, label, local_count, grad_ref, loss_ref, at):
    feat_width = xs[0].shape[1]
    codes = [x[:, feat_width:].astype(jnp.float32) for x in xs[1::2] for _ in range(2)]
    codes = jnp.concatenate(codes, axis=0)
    count = codes.shape[0]
    lane = lax.broadcasted_iota(jnp.int32, codes.shape, 1)
    row = lax.broadcasted_iota(jnp.int32, codes.shape, 0)
    lane = lane - jnp.where((row // xs[0].shape[0]) % 2 == 1, lanes // 2, 0)
    label_count = scores.shape[1] // local_count
    label_ids = lax.broadcasted_iota(jnp.int32, (count, label_count), 1) + 1
    label_ids = label_ids.astype(jnp.float32)
    loss = None
    for cluster in range(local_count):
        span = slice(cluster * label_count, (cluster + 1) * label_count)
        mine = lane == label * local_count + cluster
        code = jnp.sum(jnp.where(mine, codes, 0.0), axis=1, keepdims=True)
        logits = scores[:, span] * inv_temp
        hit = label_ids == code
        decay = jnp.exp(-jnp.abs(logits))
        each = jnp.maximum(logits, 0.0) + jnp.log1p(decay) - jnp.where(hit, logits, 0.0)
        share = jnp.where(logits >= 0.0, 1.0, decay) / (1.0 + decay)
        valid = code > 0.0
        grad = (share - jnp.where(hit, 1.0, 0.0)) * (inv_temp * grad_scale)
        grad_ref[span, at : at + count] = jnp.where(valid, grad, 0.0).T.astype(jnp.bfloat16)
        sums = jnp.where(valid, jnp.sum(each, axis=1, keepdims=True), 0.0)
        loss = sums if loss is None else loss + sums
    loss_ref[:, at : at + count] = jnp.broadcast_to(loss, (count, lanes)).T[0:1]


def stage_kernel(groups, places, depth, local_count, offsets, adds, *refs):
    take = iter(refs)

    def some(count):
        return [next(take) for _ in range(count)]

    (where_ref,) = some(1)
    ins = some(sum(groups) + len(places) + adds)
    next_ref, grad_ref, loss_ref = some(3)
    outs = some(len(offsets) * (local_count if adds else 1))
    xs, ws, sums = some(sum(groups)), some(len(places)), some(adds)
    (sems,), totals = some(1), some(1 - adds)
    me, label = where_ref[0], where_ref[1]
    next_ref[0] = me
    next_ref[1] = label
    copies = load(ins, xs + ws + sums, sems)
    weight_copies = copies[len(xs) : len(xs) + len(ws)]
    first, at = 0, 0
    for size in groups:
        for copy in copies[first : first + size]:
            copy.wait()
        group = xs[first : first + size]
        scores = row_scores(me, group, ws, weight_copies, places, depth)
        weight_copies = [None] * len(ws)
        row_terms(scores, group, label, local_count, grad_ref, loss_ref, at)
        first, at = first + size, at + scores.shape[0]
    for copy in copies[len(xs) + len(ws) :]:
        copy.wait()
    grads = grad_ref[...]
    tile = 256
    for place, offset in enumerate(offsets):
        for step in range(depth // tile):
            start = pl.multiple_of((me ^ offset) * depth + step * tile, tile)
            span = slice(step * tile, (step + 1) * tile)
            rows = jnp.concatenate([x[:, pl.ds(start, tile)] for x in xs], axis=0)
            total = jnp.dot(grads, rows, preferred_element_type=jnp.float32)
            if not adds:
                totals[0][place, :, span] = total
                continue
            total = total + sums[0][:, span]
            width = total.shape[0] // local_count
            for cluster in range(local_count):
                part = total[cluster * width : (cluster + 1) * width]
                outs[place * local_count + cluster][:, span] = part.astype(jnp.bfloat16)
        if not adds:
            pltpu.make_async_copy(totals[0].at[place], outs[place], sems.at[place]).start()
    if not adds:
        for place, out in enumerate(outs):
            pltpu.make_async_copy(totals[0].at[place], out, sems.at[place]).wait()


any_space = pl.BlockSpec(memory_space=pl.ANY)
whole = pl.BlockSpec(memory_space=pltpu.VMEM)
scalar = pl.BlockSpec(memory_space=pltpu.SMEM)


def stage_call(where, groups, ws, places, local_count, offsets):
    xs = [x for group in groups for x in group]
    rows = sum(x.shape[0] for x in xs)
    feat_width = xs[0].shape[1]
    depth, columns = ws[0].shape
    sums = ()
    inputs = [*xs, *ws, *sums]
    scratch = [pltpu.VMEM(array.shape, array.dtype) for array in inputs]
    scratch.append(pltpu.SemaphoreType.DMA((len(inputs),)))
    if sums:
        part = jax.ShapeDtypeStruct((columns // local_count, depth), jnp.bfloat16)
        outs = [part] * (local_count * len(offsets))
    else:
        outs = [jax.ShapeDtypeStruct((columns, depth), jnp.float32)] * len(offsets)
        scratch.append(pltpu.VMEM((len(offsets), columns, depth), jnp.float32))
    return pl.pallas_call(
        functools.partial(
            stage_kernel,
            tuple(len(group) for group in groups),
            places,
            depth,
            local_count,
            offsets,
            len(sums),
        ),
        out_shape=(
            jax.ShapeDtypeStruct((2,), jnp.int32),
            jax.ShapeDtypeStruct((columns, rows), jnp.bfloat16),
            jax.ShapeDtypeStruct((1, rows), jnp.float32),
            *outs,
        ),
        in_specs=[scalar] + [any_space] * len(inputs),
        out_specs=(scalar, whole, whole) + ((whole,) if sums else (any_space,)) * len(outs),
        scratch_shapes=scratch,
        compiler_params=pltpu.CompilerParams(vmem_limit_bytes=kernel_vmem),
        cost_estimate=pl.CostEstimate(
            flops=2 * rows * columns * (feat_width + depth * len(offsets)),
            bytes_accessed=2 * (rows + columns) * feat_width + 4 * columns * depth * len(offsets),
            transcendentals=2 * rows * columns,
        ),
        name="stage",
    )(where, *inputs)


def grad_tiles(me, offset, xs, grads, sums, depth):
    tile = 256
    for step in range(depth // tile):
        start = pl.multiple_of((me ^ offset) * depth + step * tile, tile)
        span = slice(step * tile, (step + 1) * tile)
        rows = jnp.concatenate([x[:, pl.ds(start, tile)] for x in xs], axis=0)
        total = jnp.dot(grads, rows, preferred_element_type=jnp.float32)
        yield span, total + sums[:, span]


def last_kernel(blocks, places, depth, local_count, offset, where_ref, *refs):
    xs, ws, refs = refs[:blocks], refs[blocks : blocks + len(places)], refs[blocks + len(places) :]
    sums, next_ref, grad_ref, loss_ref, *outs = refs
    me, label = where_ref[0], where_ref[1]
    next_ref[0] = me
    next_ref[1] = label
    scores = row_scores(me, xs, ws, [None] * len(ws), places, depth)
    row_terms(scores, xs, label, local_count, grad_ref, loss_ref, 0)
    for span, total in grad_tiles(me, offset, xs, grad_ref[...], sums, depth):
        width = total.shape[0] // local_count
        for cluster, out in enumerate(outs):
            out[:, span] = total[cluster * width : (cluster + 1) * width].astype(out.dtype)


def last_call(where, xs, ws, places, local_count, offset, sums):
    rows = sum(x.shape[0] for x in xs)
    feat_width = xs[0].shape[1]
    depth, columns = ws[0].shape
    return pl.pallas_call(
        functools.partial(last_kernel, len(xs), places, depth, local_count, offset),
        out_shape=(
            jax.ShapeDtypeStruct((2,), jnp.int32),
            jax.ShapeDtypeStruct((columns, rows), jnp.bfloat16),
            jax.ShapeDtypeStruct((1, rows), jnp.float32),
        )
        + (jax.ShapeDtypeStruct((columns // local_count, depth), jnp.bfloat16),) * local_count,
        in_specs=[scalar] + [whole] * (len(xs) + len(ws) + 1),
        out_specs=(scalar,) + (whole,) * (2 + local_count),
        compiler_params=pltpu.CompilerParams(vmem_limit_bytes=16 << 20),
        cost_estimate=pl.CostEstimate(
            flops=2 * rows * columns * (feat_width + depth),
            bytes_accessed=2 * (rows + columns) * feat_width + 6 * columns * depth,
            transcendentals=2 * rows * columns,
        ),
        name="last",
    )(where, *xs, *ws, sums)


def near_kernel(blocks, where_ref, *refs):
    ins, (grads, next_ref, near_x, near_y, on_x, on_y, own) = refs[: blocks + 3], refs[
        blocks + 3 : blocks + 10
    ]
    held, sems = refs[blocks + 10 : -1], refs[-1]
    me = where_ref[0]
    next_ref[0] = me
    next_ref[1] = where_ref[1]
    copies = load(ins, held, sems)
    xs, sums = held[:blocks], held[blocks:]
    for copy in copies[: blocks + 1]:
        copy.wait()
    grads = grads[...]
    width, depth = near_x.shape
    for span, total in grad_tiles(me, 1, xs, grads, sums[0], depth):
        near_x[:, span] = total[:width].astype(near_x.dtype)
        on_x[:, span] = total[width:]
    copies[blocks + 1].wait()
    for span, total in grad_tiles(me, 2, xs, grads, sums[1], depth):
        on_y[:, span] = total[:width]
        near_y[:, span] = total[width:].astype(near_y.dtype)
    copies[blocks + 2].wait()
    for span, total in grad_tiles(me, 0, xs, grads, sums[2], depth):
        own[:, span] = total


def near_call(where, xs, grads, sums):
    columns, depth = sums[0].shape
    rows = grads.shape[1]
    half = (columns // 2, depth)
    inputs = (*xs, sums[1], sums[2], sums[0])
    return pl.pallas_call(
        functools.partial(near_kernel, len(xs)),
        out_shape=(
            jax.ShapeDtypeStruct((2,), jnp.int32),
            jax.ShapeDtypeStruct(half, jnp.bfloat16),
            jax.ShapeDtypeStruct(half, jnp.bfloat16),
            jax.ShapeDtypeStruct(half, jnp.float32),
            jax.ShapeDtypeStruct(half, jnp.float32),
            jax.ShapeDtypeStruct((columns, depth), jnp.float32),
        ),
        in_specs=[scalar] + [any_space] * len(inputs) + [whole],
        out_specs=(scalar,) + (whole,) * 5,
        scratch_shapes=[
            *(pltpu.VMEM(array.shape, array.dtype) for array in inputs),
            pltpu.SemaphoreType.DMA((len(inputs),)),
        ],
        compiler_params=pltpu.CompilerParams(vmem_limit_bytes=24 << 20),
        cost_estimate=pl.CostEstimate(
            flops=6 * rows * columns * depth,
            bytes_accessed=22 * columns * depth,
            transcendentals=0,
        ),
        name="near",
    )(where, *inputs, grads)


def join_kernel(on_x, far_y, on_y, far_x, out_x, out_y):
    out_x[...] = (on_x[...] + far_y[...].astype(jnp.float32)).astype(out_x.dtype)
    out_y[...] = (on_y[...] + far_x[...].astype(jnp.float32)).astype(out_y.dtype)


def join_call(on_x, far_y, on_y, far_x):
    part = jax.ShapeDtypeStruct(far_x.shape, far_x.dtype)
    return pl.pallas_call(
        join_kernel,
        out_shape=(part, part),
        in_specs=[whole] * 4,
        out_specs=(whole, whole),
        compiler_params=pltpu.CompilerParams(vmem_limit_bytes=4 << 20),
        name="join",
    )(on_x, far_y, on_y, far_x)


def base_kernel(own, got_x, got_y, out):
    width = got_x.shape[0]
    out[:width] = own[:width] + got_x[...].astype(jnp.float32)
    out[width:] = own[width:] + got_y[...].astype(jnp.float32)


def base_call(own, got_x, got_y):
    return pl.pallas_call(
        base_kernel,
        out_shape=jax.ShapeDtypeStruct(own.shape, own.dtype),
        in_specs=[whole] * 3,
        out_specs=whole,
        compiler_params=pltpu.CompilerParams(vmem_limit_bytes=4 << 20),
        name="base",
    )(own, got_x, got_y)


def final_kernel(base, pass_y, pass_x, out):
    tile = 256
    width = pass_y.shape[0]
    for step in range(out.shape[0] // tile):
        span = slice(step * tile, (step + 1) * tile)
        first = base[:width, span] + pass_y[:, span].astype(jnp.float32)
        second = base[width:, span] + pass_x[:, span].astype(jnp.float32)
        out[span, :width] = first.T.astype(out.dtype)
        out[span, width:] = second.T.astype(out.dtype)


def final_call(base, pass_y, pass_x):
    columns, depth = base.shape
    return pl.pallas_call(
        final_kernel,
        out_shape=jax.ShapeDtypeStruct((depth, columns), jnp.bfloat16),
        in_specs=[whole] * 3,
        out_specs=whole,
        compiler_params=pltpu.CompilerParams(vmem_limit_bytes=4 << 20),
        name="final",
    )(base, pass_y, pass_x)


def tie(*values):
    return lax.optimization_barrier(values)


def ring_body(samples, weight, matches, positives):
    row_count, feat_width = samples.shape
    depth, local_count, label_count = weight.shape
    groups = lax.axis_size("label")
    pick_count = matches.shape[1]
    clusters = groups * local_count
    dp = lax.axis_index("dp")
    label = lax.axis_index("label")
    where = jnp.stack([dp, label]).astype(jnp.int32)

    chips = groups // 2
    hop = [(z * 2 + c, ring_next[z] * 2 + c) for z in range(chips) for c in range(2)]
    swap = [(i, i ^ 1) for i in range(groups)]
    along_x = [(i, i ^ 1) for i in range(4)]
    along_y = [(i, i ^ 2) for i in range(4)]

    part = row_count // halves
    where, coded = pack_call(where, samples[part:], matches, positives)
    blocks = [samples[:part], coded]
    flat, where = tie(weight.reshape(depth, local_count * label_count), where)
    half = depth // 2

    def hops(blocks):
        return [lax.ppermute(block, "label", hop) for block in blocks]

    mine = [blocks, hops(blocks)]
    w_x = lax.ppermute(flat, "dp", along_x)
    w_y = lax.ppermute(flat, "dp", along_y)
    mine[1][0], w_x, w_y = tie(mine[1][0], w_x, w_y)
    mine.append(hops(mine[1]))
    far_x = lax.ppermute(w_x[:half], "dp", along_y)
    far_y = lax.ppermute(w_y[half:], "dp", along_x)
    mine[2][0], far_x, far_y = tie(mine[2][0], far_x, far_y)
    last = hops(mine[2])
    ws = [flat, w_x, w_y, far_x, far_y]
    places = ((0, 0), (1, 0), (2, 0), (3, 0), (3, half))

    def with_mates(blocks):
        return blocks + [lax.ppermute(block, "label", swap) for block in blocks]

    early = [with_mates(blocks) for blocks in mine]

    offsets = (3, 1, 2, 0)
    token, _, loss, *sums = stage_call(where, early, ws, places, local_count, offsets)
    token, *last = tie(token, *last)
    losses = [loss]
    sums = dict(zip(offsets, sums))

    xs = with_mates(last)
    token, grads, loss, far_0, far_1 = last_call(token, xs, ws, places, local_count, 3, sums[3])
    losses.append(loss)
    far_x = lax.ppermute(far_0, "dp", along_x)
    far_y = lax.ppermute(far_1, "dp", along_y)
    token, near_x, near_y, on_x, on_y, own = near_call(token, xs, grads, sums)
    got_x = lax.ppermute(near_x, "dp", along_x)
    got_y = lax.ppermute(near_y, "dp", along_y)
    on_x, on_y = join_call(on_x, far_y, on_y, far_x)

    order = []
    for z in range(chips):
        for c in range(2):
            at, steps = z, []
            for _ in range(chips):
                steps.append([at * 2 + c, at * 2 + 1 - c])
                at = ring_prev[at]
            order.append(steps)
    order = jnp.array(order, jnp.int32)[label]
    by_step, on_x, on_y = tie(
        jnp.concatenate(losses, axis=1).reshape(groups, row_count), on_x, on_y
    )
    pass_x = lax.ppermute(on_x, "dp", along_x)
    pass_y = lax.ppermute(on_y, "dp", along_y)
    total = jnp.zeros((groups, row_count), jnp.float32)
    total = total.at[order.reshape(-1)].set(by_step)
    returned = lax.all_to_all(total, "label", split_axis=0, concat_axis=0, tiled=True)
    sample_loss = jnp.sum(returned, axis=0) / (pick_count * label_count)

    weight_grad = final_call(base_call(own, got_x, got_y), pass_y, pass_x)
    weight_grad = weight_grad.reshape(depth, local_count, label_count)
    return (weight_grad, sample_loss)


def body(samples, weight, matches, positives):
    if (lax.axis_size("dp"), lax.axis_size("label"), weight.shape[1]) == (4, 8, 2):
        return ring_body(samples, weight, matches, positives)
    return slot_body(samples, weight, matches, positives)


def solution(mesh):
    placed = (
        P(("dp", "label"), None),
        P("dp", "label", None),
        P(("dp", "label"), None),
        P(("dp", "label"), None),
    )
    return jax.shard_map(
        body,
        mesh=mesh,
        in_specs=placed,
        out_specs=(P("dp", "label", None), P(("dp", "label"))),
        check_vma=False,
    )
```
